32 devices in a mesh: batch: 16 (over z, y, core), seq: 2 (over x).
Axes of the slice: x: 2, y: 2, z: 4, core: 2. Of those that a mesh axis runs over, the one named last changes fastest.
Arguments:
- inputs: bfloat16 [64, 512, 768], P(('batch', 'seq')), may hold values from -6 to 6
- lengths: int32 [64], P(('batch', 'seq')), may hold values from 1 to 512, 24576 in all
- cotangent: bfloat16 [64, 512, 768], P(('batch', 'seq')), may hold values from -6 to 6
- ln1_gain: bfloat16 [768], P(('batch', 'seq')), may hold values from 0.099609375 to 1.8984375
- ln1_bias: bfloat16 [768], P(('batch', 'seq')), may hold values from -1.75 to 1.75
- qkv_weight: bfloat16 [768, 2304], P(('batch', 'seq')), may hold values from -0.21875 to 0.21875
- q_bias: bfloat16 [768], P(('batch', 'seq')), may hold values from -1.75 to 1.75
- v_bias: bfloat16 [768], P(('batch', 'seq')), may hold values from -1.75 to 1.75
- out_weight: bfloat16 [768, 768], P(('batch', 'seq')), may hold values from -2.5 to 2.5
- out_bias: bfloat16 [768], P(('batch', 'seq')), may hold values from -1.75 to 1.75
- ln2_gain: bfloat16 [768], P(('batch', 'seq')), may hold values from 0.099609375 to 1.8984375
- ln2_bias: bfloat16 [768], P(('batch', 'seq')), may hold values from -1.75 to 1.75
- up_weight: bfloat16 [768, 3072], P(('batch', 'seq')), may hold values from -0.21875 to 0.21875
- up_bias: bfloat16 [3072], P(('batch', 'seq')), may hold values from -1.75 to 1.75
- down_weight: bfloat16 [3072, 768], P(('batch', 'seq')), may hold values from -0.109375 to 0.109375
- down_bias: bfloat16 [768], P(('batch', 'seq')), may hold values from -1.75 to 1.75
Outputs:
- activations: bfloat16 [64, 512, 768], P(('batch', 'seq'))
- input_grad: float32 [64, 512, 768], P(('batch', 'seq'))
- ln1_gain_grad: float32 [768], P(('batch', 'seq'))
- ln1_bias_grad: float32 [768], P(('batch', 'seq'))
- qkv_weight_grad: float32 [768, 2304], P(('batch', 'seq'))
- q_bias_grad: float32 [768], P(('batch', 'seq'))
- v_bias_grad: float32 [768], P(('batch', 'seq'))
- out_weight_grad: float32 [768, 768], P(('batch', 'seq'))
- out_bias_grad: float32 [768], P(('batch', 'seq'))
- ln2_gain_grad: float32 [768], P(('batch', 'seq'))
- ln2_bias_grad: float32 [768], P(('batch', 'seq'))
- up_weight_grad: float32 [768, 3072], P(('batch', 'seq'))
- up_bias_grad: float32 [3072], P(('batch', 'seq'))
- down_weight_grad: float32 [3072, 768], P(('batch', 'seq'))
- down_bias_grad: float32 [768], P(('batch', 'seq'))
The draws below stay inside these ranges and needn't reach their ends.
Inputs may be any that keep to these rules, and one draw needn't show every extreme that they name: The first lengths[s] patches of sequence s are valid keys, the others are masked; the longest sequence has all 512 patches valid.
All inputs are finite; a program needn't handle non-finite values. No bound on the sum of `lengths` on one device may be relied on, other than what follows from the above.
Results may differ from the reference program's by a relative error of at most 0.0099.
Values may be sent and summed in bfloat16 or wider, within the bound.
A program may use at most 192 MiB of HBM per device.

```python
import math
import jax
import jax.numpy as jnp
import numpy as np
from jax import lax

D = 768
FF = 3072
HEADS = 12
HEAD_DIM = 64
LEN = 512
SEQS = 64


def with_spikes(entries, stream_key, source, target, parts, factor):
    owner, partner = [(jnp.arange(entries.shape[dim]) // (entries.shape[dim] // parts)).reshape([-1 if axis == dim else 1 for axis in range(entries.ndim)]) for dim in (source, target)]
    chosen = jax.random.permutation(stream_key, parts)[partner]
    strong = (owner == chosen) | (owner == (partner + parts // 2) % parts)
    return jnp.where(strong, factor * entries, entries)


def block_scale(stream_key, dims, cuts, smallest, high):
    factor_of, own = 1.0, jax.random.fold_in(stream_key, 6)
    for position, blocks in cuts:
        steps = jnp.exp(jax.random.uniform(jax.random.fold_in(own, position), (blocks,), jnp.float32, smallest / len(cuts), high / len(cuts)))
        factor_of = factor_of * jnp.repeat(steps, dims[position] // blocks).reshape([-1 if axis == position else 1 for axis in range(len(dims))])
    return factor_of


def profile(number_of, total, bound, slope):
    portions = [(1 << 20) // math.isqrt(standing ** slope) + 1 for standing in range(2, number_of + 1)]
    spare, given = total - bound - (number_of - 1), [1] * (number_of - 1)
    while spare > 0:
        candidates = [i for i in range(number_of - 1) if given[i] < bound]
        pool, remaining = sum([portions[i] for i in candidates]), spare
        for i in candidates:
            extra = min(bound - given[i], max(1, remaining * portions[i] // pool), spare)
            given[i] = given[i] + extra
            spare = spare - extra
    return np.array([bound] + given)


def uneven_parts(own_key, count, total, limit, lean):
    if count == 2:
        one = jax.random.randint(own_key, (), max(1, total - limit), min(limit, total - 1) + 1)
        return jnp.stack([one, total - one])
    sizes = jnp.asarray(profile(count, total, limit, lean), jnp.int32)
    pairs = (count - 1) // 2
    source_of, sink = sizes[1:1 + 2 * pairs:2], sizes[2:2 + 2 * pairs:2]
    slack = jnp.minimum(source_of - 1, limit - sink)
    shifted = jax.random.randint(jax.random.fold_in(own_key, 1), (pairs,), 0, 1 << 20) % (slack + 1)
    sizes = sizes.at[1:1 + 2 * pairs:2].set(source_of - shifted).at[2:2 + 2 * pairs:2].set(sink + shifted)
    return sizes[jax.random.permutation(jax.random.fold_in(own_key, 2), count)]


def normal_values(own_key, shape, width, bound, split=(), dtype=jnp.bfloat16):
    drawn = jax.random.normal(own_key, shape, jnp.float32) * width
    if len(split) > 0:
        drawn = block_scale(own_key, shape, split, -0.22, 0.18) * drawn
    return jnp.clip(drawn, min=-bound, max=bound).astype(dtype)


def noise_with(own_key, shape, spread, limit, split, heavy, kind=jnp.bfloat16):
    entries = spread * jax.random.normal(own_key, shape, jnp.float32)
    if split:
        entries = entries * block_scale(own_key, shape, split, -0.22, 0.18)
    return jnp.clip(with_spikes(entries, jax.random.fold_in(own_key, 3), *heavy), -limit, limit).astype(kind)


def setup_inputs(seed: int = 0) -> dict:
    keys = jax.random.split(jax.random.key(seed), 17)
    return {
        "inputs": noise_with(keys[0], (SEQS, LEN, D), 1.0, 6.0, ((0, 32),), (0, 2, 32, 2.75)),
        "lengths": uneven_parts(keys[1], SEQS, SEQS * LEN * 3 // 4, LEN, 0).astype(jnp.int32),
        "cotangent": normal_values(keys[2], (SEQS, LEN, D), 1.0, 6.0, ((0, 32),)),
        "ln1_gain": jnp.clip(1.0 + 0.18 * jax.random.normal(keys[3], (D,), jnp.float32), 0.099609375, 1.8984375).astype(jnp.bfloat16),
        "ln1_bias": normal_values(keys[4], (D,), 0.3, 1.75, ((0, 32),)),
        "qkv_weight": normal_values(keys[5], (D, 3 * D), D ** -0.5, 0.21875, ((0, 32),)),
        "q_bias": normal_values(keys[6], (D,), 0.3, 1.75, ((0, 32),)),
        "v_bias": normal_values(keys[7], (D,), 0.3, 1.75, ((0, 32),)),
        "out_weight": normal_values(keys[8], (D, D), (D // 128) ** -0.5, 2.5, ((0, 32),)),
        "out_bias": normal_values(keys[9], (D,), 0.3, 1.75, ((0, 32),)),
        "ln2_gain": jnp.clip(1.0 + 0.18 * jax.random.normal(keys[10], (D,), jnp.float32), 0.099609375, 1.8984375).astype(jnp.bfloat16),
        "ln2_bias": normal_values(keys[11], (D,), 0.3, 1.75, ((0, 32),)),
        "up_weight": normal_values(keys[12], (D, FF), D ** -0.5, 0.21875, ((0, 32),)),
        "up_bias": normal_values(keys[13], (FF,), 0.3, 1.75, ((0, 32),)),
        "down_weight": normal_values(keys[14], (FF, D), FF ** -0.5, 0.109375, ((0, 32),)),
        "down_bias": normal_values(keys[15], (D,), 0.3, 1.75, ((0, 32),)),
    }


HIGH = lax.Precision.HIGHEST
EPS = 1e-06

@jax.custom_vjp
def low(v):
    return lax.optimization_barrier(v.astype(jnp.bfloat16)).astype(jnp.float32)

@jax.custom_vjp
def low_back(v):
    return v

def low_keep(v):
    return (low(v), None)

def low_pass(kept, grad):
    return (grad,)

def back_keep(v):
    return (v, None)

def back_low(kept, grad):
    return (low(grad),)
low.defvjp(low_keep, low_pass)
low_back.defvjp(back_keep, back_low)

def layer_norm(features_in, gain_vec, shift_vec):
    centered = features_in - lax.optimization_barrier(jnp.mean(features_in, -1, keepdims=True))
    variance = lax.optimization_barrier(jnp.mean(centered * centered, -1, keepdims=True))
    return centered * lax.rsqrt(variance + EPS) * gain_vec + shift_vec

def gelu_exact(values):
    return 0.5 * values * (1.0 + lax.erf(values * 0.7071067811865476))

def product(left_side, right_side):
    return jnp.dot(left_side, right_side, precision=HIGH, preferred_element_type=jnp.float32)

def attend(seq_block):
    queries, key_rows, value_rows, length = seq_block
    query_heads = queries.reshape(LEN, HEADS, HEAD_DIM)
    key_heads = key_rows.reshape(LEN, HEADS, HEAD_DIM)
    value_heads = value_rows.reshape(LEN, HEADS, HEAD_DIM)
    scores = jnp.einsum('qhd,khd->hqk', query_heads, key_heads, precision=HIGH)
    scores = low_back(scores * HEAD_DIM ** (-0.5))
    visible = jnp.arange(LEN) < length
    scores = jnp.where(visible[None, None, :], scores, -1e+30)
    row_max = lax.optimization_barrier(jnp.max(scores, -1, keepdims=True))
    expo_terms = jnp.exp(scores - row_max)
    softmax_low = low(expo_terms / lax.optimization_barrier(jnp.sum(expo_terms, -1, keepdims=True)))
    attended = jnp.einsum('hqk,khd->qhd', softmax_low, value_heads, precision=HIGH)
    return attended.reshape(LEN, D)

def forward(x_block, param_set, length_block):
    gain_one, shift_one, qkv_full, q_shift, v_shift, out_full, out_shift, gain_two, shift_two, up_full, up_shift, down_full, down_shift = param_set
    x_rows = x_block.reshape(-1, D)
    h_one = low(layer_norm(x_rows, gain_one, shift_one))
    bias_all = jnp.concatenate([q_shift, jnp.zeros_like(q_shift), v_shift])
    qkv = low_back(low(product(h_one, qkv_full) + bias_all))
    queries = qkv[:, :D].reshape(-1, LEN, D)
    key_rows = qkv[:, D:2 * D].reshape(-1, LEN, D)
    value_rows = qkv[:, 2 * D:].reshape(-1, LEN, D)
    attended = lax.map(jax.checkpoint(attend), (queries, key_rows, value_rows, length_block))
    attended = low_back(low(attended.reshape(-1, D)))
    middle = x_rows + low_back(product(attended, out_full) + out_shift)
    h_two = low(layer_norm(middle, gain_two, shift_two))
    act_low = low(gelu_exact(low_back(product(h_two, up_full) + up_shift)))
    outputs = middle + (product(act_low, down_full) + down_shift)
    return outputs.reshape(x_block.shape)

def add_pair(first, second):
    return first + second

def reference(inputs, lengths, cotangent, ln1_gain, ln1_bias, qkv_weight, q_bias, v_bias, out_weight, out_bias, ln2_gain, ln2_bias, up_weight, up_bias, down_weight, down_bias):
    param_set = tuple((member.astype(jnp.float32) for member in (ln1_gain, ln1_bias, qkv_weight, q_bias, v_bias, out_weight, out_bias, ln2_gain, ln2_bias, up_weight, up_bias, down_weight, down_bias)))
    group_count = SEQS // 8
    x_blocks = inputs.astype(jnp.float32).reshape(group_count, 8, LEN, D)
    grad_blocks = cotangent.astype(jnp.float32).reshape(group_count, 8, LEN, D)
    length_blocks = lengths.reshape(group_count, 8)

    def group_step(totals, scan_block):
        x_block, length_block, grad_block = scan_block

        def apply_layer(x_in, param_in):
            return forward(x_in, param_in, length_block)
        outputs, back_fn = jax.vjp(apply_layer, x_block, param_set)
        x_grad, param_grads = back_fn(grad_block)
        totals = jax.tree.map(add_pair, totals, param_grads)
        return (totals, (outputs.astype(jnp.bfloat16), x_grad))
    zero_set = tuple((jnp.zeros_like(member) for member in param_set))
    totals, (out_blocks, x_grads) = lax.scan(group_step, zero_set, (x_blocks, length_blocks, grad_blocks))
    return (out_blocks.reshape(SEQS, LEN, D), x_grads.reshape(SEQS, LEN, D), totals[0], totals[1], totals[2], totals[3], totals[4], totals[5], totals[6], totals[7], totals[8], totals[9], totals[10], totals[11], totals[12])
```

```python
import functools

import jax
import jax.numpy as jnp
from jax import lax
from jax.experimental import pallas as pl
from jax.experimental.pallas import tpu as pltpu
from jax.sharding import PartitionSpec as P

D = 768
HEADS = 12
HEAD_DIM = 64


EPS = 1e-06


def layer_norm(features_in, gain_vec, shift_vec):
    centered = features_in - jnp.mean(features_in, -1, keepdims=True)
    variance = jnp.mean(centered * centered, -1, keepdims=True)
    return centered * lax.rsqrt(variance + EPS) * gain_vec + shift_vec


def gelu_exact(values):
    return 0.5 * values * (1.0 + lax.erf(values * 0.7071067811865476))


def product(left_side, right_side):
    return jnp.dot(left_side, right_side, preferred_element_type=jnp.float32)


def product_left(left_side, right_side):
    return lax.dot_general(
        left_side, right_side, (((0,), (0,)), ((), ())), preferred_element_type=jnp.float32
    )


def product_right(left_side, right_side):
    return lax.dot_general(
        left_side, right_side, (((1,), (1,)), ((), ())), preferred_element_type=jnp.float32
    )


def split_heads(matrix_rows):
    return matrix_rows.reshape(matrix_rows.shape[0], HEADS, HEAD_DIM)


def masked_scores(queries, key_rows, length):
    scores = jnp.einsum(
        "qhd,khd->hqk",
        split_heads(queries),
        split_heads(key_rows),
        preferred_element_type=jnp.float32,
    ) * HEAD_DIM ** (-0.5)
    visible = jnp.arange(key_rows.shape[0]) < length
    return jnp.where(visible[None, None, :], scores, -1e30)


def attend_forward(seq_block):
    queries, key_rows, value_rows, length = seq_block
    scores = masked_scores(queries, key_rows, length)
    row_max = jnp.max(scores, -1, keepdims=True)
    expo_terms = jnp.exp(scores - row_max)
    row_total = jnp.sum(expo_terms, -1, keepdims=True)
    softmax_low = (expo_terms / row_total).astype(jnp.bfloat16)
    attended = jnp.einsum(
        "hqk,khd->qhd", softmax_low, split_heads(value_rows), preferred_element_type=jnp.float32
    )
    return (
        attended.reshape(queries.shape[0], D).astype(jnp.bfloat16),
        row_max + jnp.log(row_total),
    )


def attend_backward(seq_block):
    queries, key_rows, value_rows, length, log_total, grad_out = seq_block
    scores = masked_scores(queries, key_rows, length)
    softmax_full = jnp.exp(scores - log_total)
    softmax_low = softmax_full.astype(jnp.bfloat16)
    grad_heads = split_heads(grad_out)
    grad_soft = jnp.einsum(
        "qhd,khd->hqk", grad_heads, split_heads(value_rows), preferred_element_type=jnp.float32
    )
    value_grad = jnp.einsum(
        "hqk,qhd->khd", softmax_low, grad_heads, preferred_element_type=jnp.float32
    )
    row_dot = jnp.sum(softmax_full * grad_soft, -1, keepdims=True)
    score_grad = (softmax_full * (grad_soft - row_dot)).astype(jnp.bfloat16)
    query_grad = jnp.einsum(
        "hqk,khd->qhd", score_grad, split_heads(key_rows), preferred_element_type=jnp.float32
    ) * HEAD_DIM ** (-0.5)
    key_grad = jnp.einsum(
        "hqk,qhd->khd", score_grad, split_heads(queries), preferred_element_type=jnp.float32
    ) * HEAD_DIM ** (-0.5)
    key_count = key_rows.shape[0]
    return (
        query_grad.reshape(queries.shape[0], D).astype(jnp.bfloat16),
        key_grad.reshape(key_count, D).astype(jnp.bfloat16),
        value_grad.reshape(key_count, D).astype(jnp.bfloat16),
    )


MESH = pl.DeviceIdType.MESH
GATHER_SEMS = 28
REDUCE_SEMS = 27


class Where:
    def __init__(self):
        batch = lax.axis_index("batch")
        self.x = x = lax.axis_index("seq")
        self.z = z = batch // 4
        self.y = y = lax.rem(batch // 2, 2)
        self.c = c = lax.rem(batch, 2)
        self.xp, self.yp = x + (1 - c) * (1 - 2 * x), y + c * (1 - 2 * y)
        self.xq, self.yq = x + c * (1 - 2 * x), y + (1 - c) * (1 - 2 * y)
        self.zf, self.zb = lax.rem(z + 5 - 2 * c, 4), lax.rem(z + 3 + 2 * c, 4)
        self.zo = lax.rem(z + 2, 4)
        self.sibling = self.device(z, y, 1 - c, x)
        self.pn = self.device(z, self.yp, c, self.xp)
        self.qn = self.device(z, self.yq, c, self.xq)
        self.fn = self.device(self.zf, y, c, x)
        self.bn = self.device(self.zb, y, c, x)

    def device(self, z, y, c, x):
        return (z * 4 + y * 2 + c, x)

    def barrier(self):
        sem = pltpu.get_barrier_semaphore()
        for dev in (self.pn, self.qn, self.fn, self.bn, self.sibling):
            pl.semaphore_signal(sem, inc=1, device_id=dev, device_id_type=MESH)
        pl.semaphore_wait(sem, 5)


class Copies:
    def __init__(self, send, recv):
        self.send, self.recv, self.kept, self.count = send, recv, {}, 0

    def start(self, key, source, target, dev):
        copy = pltpu.make_async_remote_copy(
            src_ref=source,
            dst_ref=target,
            send_sem=self.send.at[self.count],
            recv_sem=self.recv.at[self.count],
            device_id=dev,
            device_id_type=MESH,
        )
        self.count += 1
        copy.start()
        self.kept[key] = copy

    def got(self, *keys):
        for key in keys:
            self.kept[key].wait_recv()

    def drain(self):
        for copy in self.kept.values():
            copy.wait_send()


def gather_steps(w, src, full, send, recv, cut):
    cols = src.shape[1]
    low, high = pl.ds(0, cut), pl.ds(cut, cols - cut)
    z, y, c, x = w.z, w.y, w.c, w.x
    k = Copies(send, recv)
    local = pltpu.make_async_copy(src, full.at[z, y, c, x], recv.at[GATHER_SEMS - 1])

    def pass_on(key, zz, yy, xx, dev):
        block = full.at[zz, yy, c, xx, :, high]
        k.start(key, block, block, dev)

    def first():
        own = src.at[:, high]
        to = full.at[z, y, c, x, :, high]
        k.start("f", own, to, w.fn)
        k.start("b", own, to, w.bn)
        if cut:
            k.start("a1", src.at[:, low], full.at[z, y, c, x, :, low], w.pn)
            k.start("a2", src.at[:, low], full.at[z, y, c, x, :, low], w.qn)
        k.start("p0", own, to, w.pn)
        k.start("q0", own, to, w.qn)
        local.start()

    def second():
        if cut:
            k.got("a1")
            block = full.at[z, w.yp, c, w.xp, :, low]
            k.start("a3", block, block, w.qn)
        k.got("f")
        pass_on("ff", w.zb, y, x, w.fn)
        pass_on("p1", w.zb, y, x, w.pn)
        pass_on("q1", w.zb, y, x, w.qn)
        k.got("b")
        pass_on("p2", w.zf, y, x, w.pn)
        pass_on("q2", w.zf, y, x, w.qn)
        k.got("p0")
        pass_on("r0", z, w.yp, w.xp, w.qn)

    def third():
        local.wait()
        if cut:
            k.got("a2", "a3")
            block = full.at[z, :, c, :, :, low]
            k.start("af", block, block, w.fn)
            k.start("ab", block, block, w.bn)
        k.got("ff")
        pass_on("p3", w.zo, y, x, w.pn)
        pass_on("q3", w.zo, y, x, w.qn)
        k.got("p1")
        pass_on("r1", w.zb, w.yp, w.xp, w.qn)
        k.got("p2")
        pass_on("r2", w.zf, w.yp, w.xp, w.qn)

    def fourth():
        if cut:
            k.got("af")
            block = full.at[w.zb, :, c, :, :, low]
            k.start("aff", block, block, w.fn)
        k.got("p3")
        pass_on("r3", w.zo, w.yp, w.xp, w.qn)

    def fifth():
        k.got("q0", "r0", "q1", "r1", "q2", "r2")
        for key, zz in (("d0", z), ("d1", w.zb), ("d2", w.zf)):
            block = full.at[zz, :, c, :, :, high]
            k.start(key, block, block, w.sibling)

    def sixth():
        if cut:
            k.got("ab", "aff")
            block = full.at[:, :, c, :, :, low]
            k.start("da", block, block, w.sibling)
        k.got("q3", "r3")
        block = full.at[w.zo, :, c, :, :, high]
        k.start("d3", block, block, w.sibling)

    def last():
        k.got("d0", "d1", "d2", "d3")
        if cut:
            k.got("da")
        k.drain()

    return [first, second, third, fourth, fifth, sixth, last]


def reduce_scratch(rows, cols, cut, dtype):
    rest = cols - cut
    shapes = [(4, 2, 2, rows, cols), (4, 2, 2, rows, cols), (2, 4, rows, rest), (4, rows, rest), (3, rows, rest)]
    if cut:
        shapes += [(3, 2, 2, rows, cut), (3, rows, cut)]
    return [pltpu.VMEM(shape, dtype) for shape in shapes]


def reduce_steps(w, parts, out, scratch, send, recv, cut):
    rows, cols = out.shape
    held, other, from_q, from_p, from_z = scratch[:5]
    if cut:
        low_z, low_pq = scratch[5:]
    low, high = pl.ds(0, cut), pl.ds(cut, cols - cut)
    z, y, c, x = w.z, w.y, w.c, w.x
    yr, xr = 1 - y, 1 - x
    k = Copies(send, recv)
    local = pltpu.make_async_copy(parts.at[:, :, c], held, recv.at[REDUCE_SEMS - 1])
    pairs = [(a, b) for a in range(2) for b in range(2)]

    def add(target, term):
        target[...] = (target[...].astype(jnp.float32) + term[...].astype(jnp.float32)).astype(target.dtype)

    def total(mine, one, two):
        return mine.astype(jnp.float32) + one.astype(jnp.float32) + two.astype(jnp.float32)

    def add_sibling(zz, span):
        for a, b in pairs:
            add(held.at[zz, a, b, :, span], other.at[zz, a, b, :, span])

    def first():
        k.start("so", parts.at[w.zo, :, 1 - c, :, :, high], other.at[w.zo, :, :, :, high], w.sibling)
        if cut:
            k.start("sa", parts.at[:, :, 1 - c, :, :, low], other.at[:, :, :, :, low], w.sibling)
        for key, zz in (("sb", w.zf), ("sf", w.zb), ("sz", z)):
            k.start(key, parts.at[zz, :, 1 - c, :, :, high], other.at[zz, :, :, :, high], w.sibling)
        local.start()

    def to_q(key, zz):
        k.start("r" + key, held.at[zz, yr, xr, :, high], from_q.at[1, zz], w.qn)
        k.start("q" + key, held.at[zz, w.yq, w.xq, :, high], from_q.at[0, zz], w.qn)

    def second():
        local.wait()
        k.got("so")
        add_sibling(w.zo, high)
        to_q("o", w.zo)
        if cut:
            k.got("sa")
            add_sibling(w.zo, low)
            k.start("ao", held.at[w.zo, :, :, :, low], low_z.at[0], w.fn)
            add_sibling(w.zb, low)
            k.start("ab", held.at[w.zb, :, :, :, low], low_z.at[1], w.bn)
            add_sibling(w.zf, low)
            add_sibling(z, low)
        for key, zz in (("b", w.zb), ("f", w.zf), ("z", z)):
            k.got("s" + key)
            add_sibling(zz, high)
            to_q(key, zz)

    def to_p(key, zz):
        k.got("r" + key)
        add(held.at[zz, w.yp, w.xp, :, high], from_q.at[1, zz])
        k.start("p" + key, held.at[zz, w.yp, w.xp, :, high], from_p.at[zz], w.pn)

    def third():
        to_p("o", w.zo)
        if cut:
            k.got("ao")
            for a, b in pairs:
                add(held.at[w.zf, a, b, :, low], low_z.at[0, a, b])
            k.start("af", held.at[w.zf, :, :, :, low], low_z.at[2], w.fn)
        to_p("f", w.zf)
        to_p("b", w.zb)
        to_p("z", z)

    def finish(key, zz):
        k.got("q" + key)
        add(held.at[zz, y, x, :, high], from_q.at[0, zz])
        k.got("p" + key)
        add(held.at[zz, y, x, :, high], from_p.at[zz])

    def fourth():
        finish("o", w.zo)
        k.start("zo", held.at[w.zo, y, x, :, high], from_z.at[0], w.fn)
        finish("f", w.zf)
        finish("b", w.zb)
        k.start("zb", held.at[w.zb, y, x, :, high], from_z.at[1], w.bn)
        finish("z", z)

    def fifth():
        if cut:
            k.got("ab", "af")
            for a, b in pairs:
                block = held.at[z, a, b, :, low]
                block[...] = total(block[...], low_z[1, a, b], low_z[2, a, b]).astype(block.dtype)
            k.start("lr", held.at[z, yr, xr, :, low], low_pq.at[0], w.qn)
            k.start("lq", held.at[z, w.yq, w.xq, :, low], low_pq.at[1], w.qn)

    def sixth():
        k.got("zo")
        add(held.at[w.zf, y, x, :, high], from_z.at[0])
        k.start("zf", held.at[w.zf, y, x, :, high], from_z.at[2], w.fn)
        if cut:
            k.got("lr")
            add(held.at[z, w.yp, w.xp, :, low], low_pq.at[0])
            k.start("lp", held.at[z, w.yp, w.xp, :, low], low_pq.at[2], w.pn)

    def seventh():
        if cut:
            k.got("lq", "lp")
            out[:, low] = total(held[z, y, x, :, low], low_pq[1], low_pq[2])
        k.got("zb", "zf")
        out[:, high] = total(held[z, y, x, :, high], from_z[1], from_z[2])

    return [first, second, third, fourth, fifth, sixth, seventh, k.drain]

GRID = (4, 2, 2, 2)
VECTORS = 9
TILE = (16, 128)


def cut_of(cols):
    return max(128, (cols * 2 // 9 + 64) // 128 * 128) if cols > 128 else 0


def gather_all(*shards_in):
    count = len(shards_in)
    cuts = [cut_of(a.shape[1]) for a in shards_in]

    def body(*refs):
        sources, fulls, (send, recv) = refs[:count], refs[count : 2 * count], refs[2 * count :]
        w = Where()
        w.barrier()
        plans = [
            gather_steps(w, sources[i], fulls[i], send.at[i], recv.at[i], cuts[i]) for i in range(count)
        ]
        for phase in zip(*plans):
            for step in phase:
                step()

    hbm = pl.BlockSpec(memory_space=pltpu.HBM)
    fulls = pl.pallas_call(
        body,
        out_shape=[jax.ShapeDtypeStruct(GRID + a.shape, a.dtype) for a in shards_in],
        in_specs=[hbm] * count,
        out_specs=[hbm] * count,
        scratch_shapes=[pltpu.SemaphoreType.DMA((count, GATHER_SEMS))] * 2,
        compiler_params=pltpu.CompilerParams(collective_id=0, has_side_effects=True),
        name="gather",
    )(*shards_in)
    return [f.reshape(-1, f.shape[-1]) for f in fulls]


def reduce_all(*partials):
    count = len(partials)
    shapes = [(p.shape[0] // 32, p.shape[1]) for p in partials]
    cuts = [cut_of(s[1]) for s in shapes]
    scratch = [reduce_scratch(*shapes[i], cuts[i], partials[i].dtype) for i in range(count)]
    ends = [0]
    for group in scratch:
        ends.append(ends[-1] + len(group))

    def body(*refs):
        parts, outs, (send, recv) = refs[:count], refs[count : 2 * count], refs[2 * count : 2 * count + 2]
        room = refs[2 * count + 2 :]
        w = Where()
        w.barrier()
        plans = [
            reduce_steps(
                w, parts[i], outs[i], room[ends[i] : ends[i + 1]], send.at[i], recv.at[i], cuts[i]
            )
            for i in range(count)
        ]
        for phase in zip(*plans):
            for step in phase:
                step()

    hbm = pl.BlockSpec(memory_space=pltpu.HBM)
    vmem = pl.BlockSpec(memory_space=pltpu.VMEM)
    return pl.pallas_call(
        body,
        out_shape=[jax.ShapeDtypeStruct(s, jnp.float32) for s in shapes],
        in_specs=[hbm] * count,
        out_specs=[vmem] * count,
        scratch_shapes=[pltpu.SemaphoreType.DMA((count, REDUCE_SEMS))] * 2 + sum(scratch, []),
        compiler_params=pltpu.CompilerParams(
            collective_id=1, has_side_effects=True, vmem_limit_bytes=48 << 20
        ),
        name="reduce",
    )(*[p.reshape(GRID + shapes[i]) for i, p in enumerate(partials)])


def pack_rows(vectors, dtype):
    rows = [jnp.pad(v.astype(dtype), ((0, 0), (0, TILE[1] - v.shape[1]))) for v in vectors]
    rows += [jnp.zeros((rows[0].shape[0], TILE[1]), dtype)] * (TILE[0] - len(rows))
    return jnp.stack(rows, 1).reshape(-1, TILE[1])


def unpack_rows(tiles, widths):
    tiles = tiles.reshape(-1, *TILE)
    return [tiles[:, i, :width].reshape(-1) for i, width in enumerate(widths)]


def collect(params, devices):
    axes = ("batch", "seq")
    if devices != 32:
        return tuple(lax.all_gather(p, axes, axis=0, tiled=True) for p in params)
    matrices = [p for p in params if p.ndim == 2]
    vectors = [p for p in params if p.ndim == 1]
    fulls = gather_all(*matrices, pack_rows([v[None] for v in vectors], jnp.bfloat16))
    whole = iter(fulls[:-1])
    parts = iter(unpack_rows(fulls[-1], [v.shape[0] for v in vectors]))
    return tuple(next(whole) if p.ndim == 2 else next(parts) for p in params)


def distribute(grads, devices):
    axes = ("batch", "seq")
    if devices != 32:
        return tuple(
            lax.psum_scatter(g.astype(jnp.float32), axes, scatter_dimension=0, tiled=True) for g in grads
        )
    matrices = [g.astype(jnp.bfloat16) for g in grads if g.ndim == 2]
    vectors = [g.reshape(devices, -1) for g in grads if g.ndim == 1]
    sums = reduce_all(*matrices, pack_rows(vectors, jnp.float32))
    whole = iter(sums[:-1])
    parts = iter(unpack_rows(sums[-1], [v.shape[1] for v in vectors]))
    return tuple(next(whole) if g.ndim == 2 else next(parts) for g in grads)


def shards(
    devices,
    inputs,
    lengths,
    cotangent,
    ln1_gain,
    ln1_bias,
    qkv_weight,
    q_bias,
    v_bias,
    out_weight,
    out_bias,
    ln2_gain,
    ln2_bias,
    up_weight,
    up_bias,
    down_weight,
    down_bias,
):
    gathered = collect(
        (
            ln1_gain,
            ln1_bias,
            qkv_weight,
            q_bias,
            v_bias,
            out_weight,
            out_bias,
            ln2_gain,
            ln2_bias,
            up_weight,
            up_bias,
            down_weight,
            down_bias,
        ),
        devices,
    )
    gain_one = gathered[0].astype(jnp.float32)
    shift_one = gathered[1].astype(jnp.float32)
    qkv_full = gathered[2]
    q_shift = gathered[3].astype(jnp.float32)
    v_shift = gathered[4].astype(jnp.float32)
    out_full = gathered[5]
    out_shift = gathered[6].astype(jnp.float32)
    gain_two = gathered[7].astype(jnp.float32)
    shift_two = gathered[8].astype(jnp.float32)
    up_full = gathered[9]
    up_shift = gathered[10].astype(jnp.float32)
    down_full = gathered[11]
    down_shift = gathered[12].astype(jnp.float32)
    groups = inputs.shape[0]
    seq_rows = inputs.shape[1]
    x_rows = inputs.reshape(groups * seq_rows, D).astype(jnp.float32)
    norm_one, norm_one_back = jax.vjp(layer_norm, x_rows, gain_one, shift_one)
    h_one = norm_one.astype(jnp.bfloat16)
    qkv_sum = product(h_one, qkv_full)
    query_rows = (qkv_sum[:, :D] + q_shift).astype(jnp.bfloat16).reshape(groups, seq_rows, D)
    key_rows = qkv_sum[:, D : 2 * D].astype(jnp.bfloat16).reshape(groups, seq_rows, D)
    value_rows = (qkv_sum[:, 2 * D :] + v_shift).astype(jnp.bfloat16).reshape(groups, seq_rows, D)
    attended, log_total = lax.map(attend_forward, (query_rows, key_rows, value_rows, lengths))
    attended_rows = attended.reshape(groups * seq_rows, D)
    middle = x_rows + (product(attended_rows, out_full) + out_shift)
    norm_two, norm_two_back = jax.vjp(layer_norm, middle, gain_two, shift_two)
    h_two = norm_two.astype(jnp.bfloat16)
    act_full, gelu_back = jax.vjp(gelu_exact, product(h_two, up_full) + up_shift)
    act_low = act_full.astype(jnp.bfloat16)
    outputs = middle + (product(act_low, down_full) + down_shift)
    activations = outputs.astype(jnp.bfloat16).reshape(groups, seq_rows, D)
    qkv_back, out_back, up_back, down_back = qkv_full, out_full, up_full, down_full
    grad_low = cotangent.reshape(groups * seq_rows, D)
    grad_rows = grad_low.astype(jnp.float32)
    down_weight_grad = product_left(act_low, grad_low)
    down_bias_grad = jnp.sum(grad_rows, 0)
    pre_grad = gelu_back(product_right(grad_low, down_back))[0].astype(jnp.bfloat16)
    up_weight_grad = product_left(h_two, pre_grad)
    up_bias_grad = jnp.sum(pre_grad.astype(jnp.float32), 0)
    mid_norm_grad, ln2_gain_grad, ln2_bias_grad = norm_two_back(product_right(pre_grad, up_back))
    middle_grad = grad_rows + mid_norm_grad
    branch_low = middle_grad.astype(jnp.bfloat16)
    out_weight_grad = product_left(attended_rows, branch_low)
    out_bias_grad = jnp.sum(branch_low.astype(jnp.float32), 0)
    attended_grad = (
        product_right(branch_low, out_back).astype(jnp.bfloat16).reshape(groups, seq_rows, D)
    )
    query_grad, key_grad, value_grad = lax.map(
        attend_backward, (query_rows, key_rows, value_rows, lengths, log_total, attended_grad)
    )
    qkv_grad = jnp.concatenate(
        [
            query_grad.reshape(groups * seq_rows, D),
            key_grad.reshape(groups * seq_rows, D),
            value_grad.reshape(groups * seq_rows, D),
        ],
        axis=1,
    )
    qkv_weight_grad = product_left(h_one, qkv_grad)
    column_sums = jnp.sum(qkv_grad.astype(jnp.float32), 0)
    q_bias_grad = column_sums[:D]
    v_bias_grad = column_sums[2 * D :]
    input_part, ln1_gain_grad, ln1_bias_grad = norm_one_back(product_right(qkv_grad, qkv_back))
    input_grad = (middle_grad + input_part).reshape(groups, seq_rows, D)
    weight_grads = distribute(
        (
            ln1_gain_grad,
            ln1_bias_grad,
            qkv_weight_grad,
            q_bias_grad,
            v_bias_grad,
            out_weight_grad,
            out_bias_grad,
            ln2_gain_grad,
            ln2_bias_grad,
            up_weight_grad,
            up_bias_grad,
            down_weight_grad,
            down_bias_grad,
        ),
        devices,
    )
    return (activations, input_grad) + weight_grads


def solution(mesh):
    in_specs = (
        P(("batch", "seq"), None, None),
        P(("batch", "seq")),
        P(("batch", "seq"), None, None),
        P(("batch", "seq")),
        P(("batch", "seq")),
        P(("batch", "seq"), None),
        P(("batch", "seq")),
        P(("batch", "seq")),
        P(("batch", "seq"), None),
        P(("batch", "seq")),
        P(("batch", "seq")),
        P(("batch", "seq")),
        P(("batch", "seq"), None),
        P(("batch", "seq")),
        P(("batch", "seq"), None),
        P(("batch", "seq")),
    )
    out_specs = (
        P(("batch", "seq"), None, None),
        P(("batch", "seq"), None, None),
        P(("batch", "seq")),
        P(("batch", "seq")),
        P(("batch", "seq"), None),
        P(("batch", "seq")),
        P(("batch", "seq")),
        P(("batch", "seq"), None),
        P(("batch", "seq")),
        P(("batch", "seq")),
        P(("batch", "seq")),
        P(("batch", "seq"), None),
        P(("batch", "seq")),
        P(("batch", "seq"), None),
        P(("batch", "seq")),
    )
    body = functools.partial(shards, mesh.size)
    return jax.shard_map(body, mesh=mesh, in_specs=in_specs, out_specs=out_specs, check_vma=False)
```

```python
import functools

import jax
import jax.numpy as jnp
from jax import lax
from jax.experimental import pallas as pl
from jax.experimental.pallas import tpu as pltpu
from jax.sharding import PartitionSpec as P


D = 768
HEADS = 12
HEAD_DIM = 64


EPS = 1e-06


MESH = pl.DeviceIdType.MESH
GATHER_SEMS = 28
REDUCE_SEMS = 27


class Where:
    def __init__(self):
        batch = lax.axis_index("batch")
        self.x = x = lax.axis_index("seq")
        self.z = z = batch // 4
        self.y = y = lax.rem(batch // 2, 2)
        self.c = c = lax.rem(batch, 2)
        self.xp, self.yp = x + (1 - c) * (1 - 2 * x), y + c * (1 - 2 * y)
        self.xq, self.yq = x + c * (1 - 2 * x), y + (1 - c) * (1 - 2 * y)
        self.zf, self.zb = lax.rem(z + 5 - 2 * c, 4), lax.rem(z + 3 + 2 * c, 4)
        self.zo = lax.rem(z + 2, 4)
        self.sibling = self.device(z, y, 1 - c, x)
        self.pn = self.device(z, self.yp, c, self.xp)
        self.qn = self.device(z, self.yq, c, self.xq)
        self.fn = self.device(self.zf, y, c, x)
        self.bn = self.device(self.zb, y, c, x)

    def device(self, z, y, c, x):
        return (z * 4 + y * 2 + c, x)

    def barrier(self):
        sem = pltpu.get_barrier_semaphore()
        for dev in (self.pn, self.qn, self.fn, self.bn, self.sibling):
            pl.semaphore_signal(sem, inc=1, device_id=dev, device_id_type=MESH)
        pl.semaphore_wait(sem, 5)


class Copies:
    def __init__(self, send, recv):
        self.send, self.recv, self.kept, self.count = send, recv, {}, 0

    def start(self, key, source, target, dev):
        copy = pltpu.make_async_remote_copy(
            src_ref=source,
            dst_ref=target,
            send_sem=self.send.at[self.count],
            recv_sem=self.recv.at[self.count],
            device_id=dev,
            device_id_type=MESH,
        )
        self.count += 1
        copy.start()
        self.kept[key] = copy

    def got(self, *keys):
        for key in keys:
            self.kept[key].wait_recv()

    def drain(self):
        for copy in self.kept.values():
            copy.wait_send()


def gather_steps(w, src, full, send, recv, cut):
    cols = src.shape[1]
    low, high = pl.ds(0, cut), pl.ds(cut, cols - cut)
    z, y, c, x = w.z, w.y, w.c, w.x
    k = Copies(send, recv)
    local = pltpu.make_async_copy(src, full.at[z, y, c, x], recv.at[GATHER_SEMS - 1])

    def pass_on(key, zz, yy, xx, dev):
        block = full.at[zz, yy, c, xx, :, high]
        k.start(key, block, block, dev)

    def first():
        own = src.at[:, high]
        to = full.at[z, y, c, x, :, high]
        k.start("f", own, to, w.fn)
        k.start("b", own, to, w.bn)
        if cut:
            k.start("a1", src.at[:, low], full.at[z, y, c, x, :, low], w.pn)
            k.start("a2", src.at[:, low], full.at[z, y, c, x, :, low], w.qn)
        k.start("p0", own, to, w.pn)
        k.start("q0", own, to, w.qn)
        local.start()

    def second():
        if cut:
            k.got("a1")
            block = full.at[z, w.yp, c, w.xp, :, low]
            k.start("a3", block, block, w.qn)
        k.got("f")
        pass_on("ff", w.zb, y, x, w.fn)
        pass_on("p1", w.zb, y, x, w.pn)
        pass_on("q1", w.zb, y, x, w.qn)
        k.got("b")
        pass_on("p2", w.zf, y, x, w.pn)
        pass_on("q2", w.zf, y, x, w.qn)
        k.got("p0")
        pass_on("r0", z, w.yp, w.xp, w.qn)

    def third():
        local.wait()
        if cut:
            k.got("a2", "a3")
            block = full.at[z, :, c, :, :, low]
            k.start("af", block, block, w.fn)
            k.start("ab", block, block, w.bn)
        k.got("ff")
        pass_on("p3", w.zo, y, x, w.pn)
        pass_on("q3", w.zo, y, x, w.qn)
        k.got("p1")
        pass_on("r1", w.zb, w.yp, w.xp, w.qn)
        k.got("p2")
        pass_on("r2", w.zf, w.yp, w.xp, w.qn)

    def fourth():
        if cut:
            k.got("af")
            block = full.at[w.zb, :, c, :, :, low]
            k.start("aff", block, block, w.fn)
        k.got("p3")
        pass_on("r3", w.zo, w.yp, w.xp, w.qn)

    def fifth():
        k.got("q0", "r0", "q1", "r1", "q2", "r2")
        for key, zz in (("d0", z), ("d1", w.zb), ("d2", w.zf)):
            block = full.at[zz, :, c, :, :, high]
            k.start(key, block, block, w.sibling)

    def sixth():
        if cut:
            k.got("ab", "aff")
            block = full.at[:, :, c, :, :, low]
            k.start("da", block, block, w.sibling)
        k.got("q3", "r3")
        block = full.at[w.zo, :, c, :, :, high]
        k.start("d3", block, block, w.sibling)

    def last():
        k.got("d0", "d1", "d2", "d3")
        if cut:
            k.got("da")
        k.drain()

    return [first, second, third, fourth, fifth, sixth, last]


def reduce_scratch(rows, cols, cut, dtype):
    rest = cols - cut
    shapes = [(4, 2, 2, rows, cols), (4, 2, 2, rows, cols), (2, 4, rows, rest), (4, rows, rest), (3, rows, rest)]
    if cut:
        shapes += [(3, 2, 2, rows, cut), (3, rows, cut)]
    return [pltpu.VMEM(shape, dtype) for shape in shapes]


def reduce_steps(w, parts, out, scratch, send, recv, cut):
    rows, cols = out.shape
    held, other, from_q, from_p, from_z = scratch[:5]
    if cut:
        low_z, low_pq = scratch[5:]
    low, high = pl.ds(0, cut), pl.ds(cut, cols - cut)
    z, y, c, x = w.z, w.y, w.c, w.x
    yr, xr = 1 - y, 1 - x
    k = Copies(send, recv)
    local = pltpu.make_async_copy(parts.at[:, :, c], held, recv.at[REDUCE_SEMS - 1])
    pairs = [(a, b) for a in range(2) for b in range(2)]

    def add(target, term):
        target[...] = (target[...].astype(jnp.float32) + term[...].astype(jnp.float32)).astype(target.dtype)

    def total(mine, one, two):
        return mine.astype(jnp.float32) + one.astype(jnp.float32) + two.astype(jnp.float32)

    def add_sibling(zz, span):
        for a, b in pairs:
            add(held.at[zz, a, b, :, span], other.at[zz, a, b, :, span])

    def first():
        k.start("so", parts.at[w.zo, :, 1 - c, :, :, high], other.at[w.zo, :, :, :, high], w.sibling)
        if cut:
            k.start("sa", parts.at[:, :, 1 - c, :, :, low], other.at[:, :, :, :, low], w.sibling)
        for key, zz in (("sb", w.zf), ("sf", w.zb), ("sz", z)):
            k.start(key, parts.at[zz, :, 1 - c, :, :, high], other.at[zz, :, :, :, high], w.sibling)
        local.start()

    def to_q(key, zz):
        k.start("r" + key, held.at[zz, yr, xr, :, high], from_q.at[1, zz], w.qn)
        k.start("q" + key, held.at[zz, w.yq, w.xq, :, high], from_q.at[0, zz], w.qn)

    def second():
        local.wait()
        k.got("so")
        add_sibling(w.zo, high)
        to_q("o", w.zo)
        if cut:
            k.got("sa")
            add_sibling(w.zo, low)
            k.start("ao", held.at[w.zo, :, :, :, low], low_z.at[0], w.fn)
            add_sibling(w.zb, low)
            k.start("ab", held.at[w.zb, :, :, :, low], low_z.at[1], w.bn)
            add_sibling(w.zf, low)
            add_sibling(z, low)
        for key, zz in (("b", w.zb), ("f", w.zf), ("z", z)):
            k.got("s" + key)
            add_sibling(zz, high)
            to_q(key, zz)

    def to_p(key, zz):
        k.got("r" + key)
        add(held.at[zz, w.yp, w.xp, :, high], from_q.at[1, zz])
        k.start("p" + key, held.at[zz, w.yp, w.xp, :, high], from_p.at[zz], w.pn)

    def third():
        to_p("o", w.zo)
        if cut:
            k.got("ao")
            for a, b in pairs:
                add(held.at[w.zf, a, b, :, low], low_z.at[0, a, b])
            k.start("af", held.at[w.zf, :, :, :, low], low_z.at[2], w.fn)
        to_p("f", w.zf)
        to_p("b", w.zb)
        to_p("z", z)

    def finish(key, zz):
        k.got("q" + key)
        add(held.at[zz, y, x, :, high], from_q.at[0, zz])
        k.got("p" + key)
        add(held.at[zz, y, x, :, high], from_p.at[zz])

    def fourth():
        finish("o", w.zo)
        k.start("zo", held.at[w.zo, y, x, :, high], from_z.at[0], w.fn)
        finish("f", w.zf)
        finish("b", w.zb)
        k.start("zb", held.at[w.zb, y, x, :, high], from_z.at[1], w.bn)
        finish("z", z)

    def fifth():
        if cut:
            k.got("ab", "af")
            for a, b in pairs:
                block = held.at[z, a, b, :, low]
                block[...] = total(block[...], low_z[1, a, b], low_z[2, a, b]).astype(block.dtype)
            k.start("lr", held.at[z, yr, xr, :, low], low_pq.at[0], w.qn)
            k.start("lq", held.at[z, w.yq, w.xq, :, low], low_pq.at[1], w.qn)

    def sixth():
        k.got("zo")
        add(held.at[w.zf, y, x, :, high], from_z.at[0])
        k.start("zf", held.at[w.zf, y, x, :, high], from_z.at[2], w.fn)
        if cut:
            k.got("lr")
            add(held.at[z, w.yp, w.xp, :, low], low_pq.at[0])
            k.start("lp", held.at[z, w.yp, w.xp, :, low], low_pq.at[2], w.pn)

    def seventh():
        if cut:
            k.got("lq", "lp")
            out[:, low] = total(held[z, y, x, :, low], low_pq[1], low_pq[2])
        k.got("zb", "zf")
        out[:, high] = total(held[z, y, x, :, high], from_z[1], from_z[2])

    return [first, second, third, fourth, fifth, sixth, seventh, k.drain]


F32, BF16 = jnp.float32, jnp.bfloat16
PAIR = 2 * HEAD_DIM


def dot_on(left, right, dim_left, dim_right):
    return lax.dot_general(
        left, right, (((dim_left,), (dim_right,)), ((), ())), preferred_element_type=F32
    )


def lane_of(rows):
    return lax.broadcasted_iota(jnp.int32, (rows, PAIR), 1)


def key_lanes(rows, length):
    lane = lax.rem(lane_of(rows), HEAD_DIM)
    position = lax.broadcasted_iota(jnp.int32, (rows, PAIR), 0)
    bias = jnp.where(position < length, 0.0, -1e30)
    return jnp.where(lane < 3, 1.0, jnp.where(lane == 3, bias, 0.0)).astype(BF16)


def row_lanes(first_head, second_head, one):
    lane = lane_of(first_head.shape[0])
    place = lax.rem(lane, HEAD_DIM)
    value = jnp.where(lane < HEAD_DIM, second_head, first_head)
    high = value.astype(BF16).astype(F32)
    rest = value - high
    middle = rest.astype(BF16).astype(F32)
    low = rest - middle
    tail = jnp.where(place == 2, low, jnp.where(place == 3, one, 0.0))
    return jnp.where(place == 0, high, jnp.where(place == 1, middle, tail)).astype(BF16)


def pair_columns(pair):
    return [pl.ds(pl.multiple_of(part * D + pair * PAIR, PAIR), PAIR) for part in range(3)]


def attend_pair(seq, pair, qkv, key_side, attended, row_side):
    here, keys_at, values_at = pair_columns(pair)
    queries = qkv[seq, :, here] * jnp.asarray(HEAD_DIM ** (-0.5), BF16)
    keys, values, side = qkv[seq, :, keys_at], qkv[seq, :, values_at], key_side[...]
    lane = lane_of(queries.shape[0])
    first = lane < HEAD_DIM
    one = (lax.rem(lane, HEAD_DIM) == 3).astype(F32).astype(BF16)
    zero = jnp.zeros_like(values)
    total, logs = None, []
    for head in range(2):
        mine = first if head == 0 else ~first
        scores = dot_on(jnp.where(mine, queries, one), jnp.where(mine, keys, side), 1, 1)
        peak = jnp.max(scores, 1, keepdims=True)
        terms = jnp.exp(scores - peak)
        weight = jnp.sum(terms, 1, keepdims=True)
        logs.append(-(peak + jnp.log(weight)))
        part = dot_on(terms.astype(BF16), jnp.where(mine, values, zero), 1, 0) * (1.0 / weight)
        total = part if total is None else total + part
    attended[seq, :, here] = total.astype(BF16)
    row_side[seq, :, here] = row_lanes(logs[0], logs[1], 1.0)


def attend_pair_back(seq, pair, qkv, key_side, attended, row_side, grad, out):
    here, keys_at, values_at = pair_columns(pair)
    scale = HEAD_DIM ** (-0.5)
    queries = qkv[seq, :, here] * jnp.asarray(scale, BF16)
    keys, values, side = qkv[seq, :, keys_at], qkv[seq, :, values_at], key_side[...]
    upper = grad[seq, :, here]
    rows = row_side[seq, :, here]
    first = lane_of(queries.shape[0]) < HEAD_DIM
    product_rows = upper.astype(F32) * attended[seq, :, here].astype(F32)
    sums = [
        jnp.sum(jnp.where(first, product_rows, 0.0), 1, keepdims=True),
        jnp.sum(jnp.where(first, 0.0, product_rows), 1, keepdims=True),
    ]
    minus = row_lanes(-sums[0], -sums[1], 0.0)
    zero = jnp.zeros_like(queries)
    results = [None] * 3
    for head in range(2):
        mine = first if head == 0 else ~first
        probs = jnp.exp(dot_on(jnp.where(mine, keys, side), jnp.where(mine, queries, rows), 1, 1))
        slope = dot_on(jnp.where(mine, values, side), jnp.where(mine, upper, minus), 1, 1)
        score_grad = (probs * slope).astype(BF16)
        parts = (
            dot_on(score_grad, jnp.where(mine, keys, zero), 0, 0),
            dot_on(score_grad, jnp.where(mine, queries, zero), 1, 0),
            dot_on(probs.astype(BF16), jnp.where(mine, upper, zero), 1, 0),
        )
        results = [new if old is None else old + new for old, new in zip(results, parts)]
    out[seq, :, here] = (results[0] * scale).astype(BF16)
    out[seq, :, keys_at] = results[1].astype(BF16)
    out[seq, :, values_at] = results[2].astype(BF16)


def attention(lengths, qkv):
    groups, rows = qkv.shape[:2]

    def body(lengths_ref, qkv_ref, attended, row_side, key_side):
        for seq in range(groups):
            key_side[...] = key_lanes(rows, lengths_ref[seq])

            @pl.loop(0, HEADS // 2)
            def _(pair):
                attend_pair(seq, pair, qkv_ref, key_side, attended, row_side)

    vmem = pl.BlockSpec(memory_space=pltpu.VMEM)
    return pl.pallas_call(
        body,
        out_shape=[jax.ShapeDtypeStruct((groups, rows, D), BF16)] * 2,
        in_specs=[pl.BlockSpec(memory_space=pltpu.SMEM), vmem],
        out_specs=[vmem] * 2,
        scratch_shapes=[pltpu.VMEM((rows, PAIR), BF16)],
        compiler_params=pltpu.CompilerParams(vmem_limit_bytes=40 << 20),
        name="attention",
    )(lengths, qkv)


def attention_back(lengths, qkv, attended, row_side, grad):
    groups, rows = qkv.shape[:2]

    def body(lengths_ref, qkv_ref, attended_ref, row_ref, grad_ref, out, key_side):
        for seq in range(groups):
            key_side[...] = key_lanes(rows, lengths_ref[seq])

            @pl.loop(0, HEADS // 2)
            def _(pair):
                attend_pair_back(seq, pair, qkv_ref, key_side, attended_ref, row_ref, grad_ref, out)

    vmem = pl.BlockSpec(memory_space=pltpu.VMEM)
    return pl.pallas_call(
        body,
        out_shape=jax.ShapeDtypeStruct(qkv.shape, BF16),
        in_specs=[pl.BlockSpec(memory_space=pltpu.SMEM)] + [vmem] * 4,
        out_specs=vmem,
        scratch_shapes=[pltpu.VMEM((rows, PAIR), BF16)],
        compiler_params=pltpu.CompilerParams(vmem_limit_bytes=40 << 20),
        name="attention_back",
    )(lengths, qkv, attended, row_side, grad)


FF_BLOCK = 512
ROW_BLOCK = 256


def normalized(rows):
    centered = rows - jnp.mean(rows, -1, keepdims=True)
    factor = lax.rsqrt(jnp.mean(centered * centered, -1, keepdims=True) + EPS)
    return centered * factor, factor


def norm_back(grad, unit, factor):
    return factor * (
        grad - jnp.mean(grad, -1, keepdims=True) - unit * jnp.mean(grad * unit, -1, keepdims=True)
    )


def ffn_body(
    attended, x, dy, out_w, vec, up_b, up_w, down_w,
    act_out, up_g, down_g, out_g, attended_g, mid_g, sums, up_sum,
    mid, h2, total, dh2, act, dpre, branch,
):
    step = pl.program_id(0)
    count = x.shape[0]
    blocks = count // ROW_BLOCK
    gain, shift = vec[5:6], vec[6:7]

    @pl.when(step == 0)
    def _():
        @pl.loop(0, blocks)
        def _(i):
            at = pl.ds(pl.multiple_of(i * ROW_BLOCK, ROW_BLOCK), ROW_BLOCK)
            rows = x[at].astype(F32) + (dot_on(attended[at], out_w[...], 1, 0) + vec[4:5])
            mid[at] = rows
            total[at] = rows + vec[7:8]
            h2[at] = (normalized(rows)[0] * gain + shift).astype(BF16)
            dh2[at] = jnp.zeros_like(rows)

    up_sum[...] = jnp.zeros_like(up_sum)

    @pl.loop(0, blocks)
    def _(i):
        at = pl.ds(pl.multiple_of(i * ROW_BLOCK, ROW_BLOCK), ROW_BLOCK)
        pre = dot_on(h2[at], up_w[...], 1, 0) + up_b[...]
        below = 0.5 * (1.0 + lax.erf(pre * 0.7071067811865476))
        low = (pre * below).astype(BF16)
        act[at] = low
        slope = below + pre * jnp.exp(-0.5 * pre * pre) * 0.3989422804014327
        grad = (dot_on(dy[at], down_w[...], 1, 1) * slope).astype(BF16)
        dpre[at] = grad
        up_sum[...] += jnp.sum(grad.astype(F32), 0, keepdims=True)
        total[at] += dot_on(low, down_w[...], 1, 0)
        dh2[at] += dot_on(grad, up_w[...], 1, 1)

    down_g[...] = dot_on(act[...], dy[...], 0, 0).astype(BF16)
    up_g[...] = dot_on(h2[...], dpre[...], 0, 0).astype(BF16)

    @pl.when(step == pl.num_programs(0) - 1)
    def _():
        sums[...] = jnp.zeros_like(sums)

        @pl.loop(0, blocks)
        def _(i):
            at = pl.ds(pl.multiple_of(i * ROW_BLOCK, ROW_BLOCK), ROW_BLOCK)
            act_out[at] = total[at].astype(BF16)
            unit, factor = normalized(mid[at])
            grad, upper = dh2[at], dy[at].astype(F32)
            rows = upper + norm_back(grad * gain, unit, factor)
            mid_g[at] = rows
            low = rows.astype(BF16)
            branch[at] = low
            attended_g[at] = dot_on(low, out_w[...], 1, 1).astype(BF16)
            for k, term in enumerate((low.astype(F32), grad * unit, grad, upper)):
                sums[k : k + 1] += jnp.sum(term, 0, keepdims=True)

        out_g[...] = dot_on(attended[...], branch[...], 0, 0).astype(BF16)


def feed_forward(attended, x, dy, out_w, vec, up_b, up_w, down_w):
    count, hidden = x.shape[0], up_w.shape[1]
    shape = jax.ShapeDtypeStruct

    def whole(*dims):
        return pl.BlockSpec(dims, lambda i: (0, 0), pipeline_mode=pl.Buffered(1))

    rows, square = whole(count, D), whole(D, D)
    by_column = pl.BlockSpec((D, FF_BLOCK), lambda i: (0, i))
    by_row = pl.BlockSpec((FF_BLOCK, D), lambda i: (i, 0))
    one_row = pl.BlockSpec((1, FF_BLOCK), lambda i: (0, i))
    vmem = pltpu.VMEM
    return pl.pallas_call(
        ffn_body,
        grid=(hidden // FF_BLOCK,),
        out_shape=[
            shape((count, D), BF16),
            shape((D, hidden), BF16),
            shape((hidden, D), BF16),
            shape((D, D), BF16),
            shape((count, D), BF16),
            shape((count, D), F32),
            shape((8, D), F32),
            shape((1, hidden), F32),
        ],
        in_specs=[rows, rows, rows, square, whole(*vec.shape), one_row, by_column, by_row],
        out_specs=[rows, by_column, by_row, square, rows, rows, whole(8, D), one_row],
        scratch_shapes=[
            vmem((count, D), F32),
            vmem((count, D), BF16),
            vmem((count, D), F32),
            vmem((count, D), F32),
            vmem((count, FF_BLOCK), BF16),
            vmem((count, FF_BLOCK), BF16),
            vmem((count, D), BF16),
        ],
        compiler_params=pltpu.CompilerParams(vmem_limit_bytes=56 << 20),
        name="feed_forward",
    )(attended, x, dy, out_w, vec, up_b, up_w, down_w)


GRID = (4, 2, 2, 2)
VECTORS = 9
TILE = (16, 128)


def cut_of(cols):
    return max(128, (cols * 2 // 9 + 64) // 128 * 128) if cols > 128 else 0


def gather_all(*shards_in):
    count = len(shards_in)
    cuts = [cut_of(a.shape[1]) for a in shards_in]

    def body(*refs):
        sources, fulls, (send, recv) = refs[:count], refs[count : 2 * count], refs[2 * count :]
        w = Where()
        w.barrier()
        plans = [
            gather_steps(w, sources[i], fulls[i], send.at[i], recv.at[i], cuts[i]) for i in range(count)
        ]
        for phase in zip(*plans):
            for step in phase:
                step()

    hbm = pl.BlockSpec(memory_space=pltpu.HBM)
    fulls = pl.pallas_call(
        body,
        out_shape=[jax.ShapeDtypeStruct(GRID + a.shape, a.dtype) for a in shards_in],
        in_specs=[hbm] * count,
        out_specs=[hbm] * count,
        scratch_shapes=[pltpu.SemaphoreType.DMA((count, GATHER_SEMS))] * 2,
        compiler_params=pltpu.CompilerParams(collective_id=0, has_side_effects=True),
        name="gather",
    )(*shards_in)
    return [f.reshape(-1, f.shape[-1]) for f in fulls]


def reduce_all(*partials):
    count = len(partials)
    shapes = [(p.shape[0] // 32, p.shape[1]) for p in partials]
    cuts = [cut_of(s[1]) for s in shapes]
    scratch = [reduce_scratch(*shapes[i], cuts[i], partials[i].dtype) for i in range(count)]
    ends = [0]
    for group in scratch:
        ends.append(ends[-1] + len(group))

    def body(*refs):
        parts, outs, (send, recv) = refs[:count], refs[count : 2 * count], refs[2 * count : 2 * count + 2]
        room = refs[2 * count + 2 :]
        w = Where()
        w.barrier()
        plans = [
            reduce_steps(
                w, parts[i], outs[i], room[ends[i] : ends[i + 1]], send.at[i], recv.at[i], cuts[i]
            )
            for i in range(count)
        ]
        for phase in zip(*plans):
            for step in phase:
                step()

    hbm = pl.BlockSpec(memory_space=pltpu.HBM)
    vmem = pl.BlockSpec(memory_space=pltpu.VMEM)
    return pl.pallas_call(
        body,
        out_shape=[jax.ShapeDtypeStruct(s, jnp.float32) for s in shapes],
        in_specs=[hbm] * count,
        out_specs=[vmem] * count,
        scratch_shapes=[pltpu.SemaphoreType.DMA((count, REDUCE_SEMS))] * 2 + sum(scratch, []),
        compiler_params=pltpu.CompilerParams(
            collective_id=1, has_side_effects=True, vmem_limit_bytes=48 << 20
        ),
        name="reduce",
    )(*[p.reshape(GRID + shapes[i]) for i, p in enumerate(partials)])


def pack_rows(vectors, dtype):
    rows = [jnp.pad(v.astype(dtype), ((0, 0), (0, TILE[1] - v.shape[1]))) for v in vectors]
    rows += [jnp.zeros((rows[0].shape[0], TILE[1]), dtype)] * (TILE[0] - len(rows))
    return jnp.stack(rows, 1).reshape(-1, TILE[1])


def unpack_rows(tiles, widths):
    tiles = tiles.reshape(-1, *TILE)
    return [tiles[:, i, :width].reshape(-1) for i, width in enumerate(widths)]


def collect(params, devices):
    axes = ("batch", "seq")
    if devices != 32:
        return tuple(lax.all_gather(p, axes, axis=0, tiled=True) for p in params)
    matrices = [p for p in params if p.ndim == 2]
    vectors = [p for p in params if p.ndim == 1]
    fulls = gather_all(*matrices, pack_rows([v[None] for v in vectors], jnp.bfloat16))
    whole = iter(fulls[:-1])
    parts = iter(unpack_rows(fulls[-1], [v.shape[0] for v in vectors]))
    return tuple(next(whole) if p.ndim == 2 else next(parts) for p in params)


def distribute(grads, devices):
    axes = ("batch", "seq")
    if devices != 32:
        return tuple(
            lax.psum_scatter(g.astype(jnp.float32), axes, scatter_dimension=0, tiled=True) for g in grads
        )
    matrices = [g.astype(jnp.bfloat16) for g in grads if g.ndim == 2]
    vectors = [g.reshape(devices, -1) for g in grads if g.ndim == 1]
    sums = reduce_all(*matrices, pack_rows(vectors, jnp.float32))
    whole = iter(sums[:-1])
    parts = iter(unpack_rows(sums[-1], [v.shape[1] for v in vectors]))
    return tuple(next(whole) if g.ndim == 2 else next(parts) for g in grads)


def shards(
    devices,
    inputs,
    lengths,
    cotangent,
    ln1_gain,
    ln1_bias,
    qkv_weight,
    q_bias,
    v_bias,
    out_weight,
    out_bias,
    ln2_gain,
    ln2_bias,
    up_weight,
    up_bias,
    down_weight,
    down_bias,
):
    gathered = collect(
        (
            ln1_gain,
            ln1_bias,
            qkv_weight,
            q_bias,
            v_bias,
            out_weight,
            out_bias,
            ln2_gain,
            ln2_bias,
            up_weight,
            up_bias,
            down_weight,
            down_bias,
        ),
        devices,
    )
    ln1_g, ln1_b, qkv_w, q_b, v_b, out_w, out_b, ln2_g, ln2_b, up_w, up_b, down_w, down_b = gathered
    groups, seq_rows = inputs.shape[:2]
    count = groups * seq_rows
    x = inputs.reshape(count, D)
    vec = jnp.stack([v.astype(F32) for v in (ln1_g, ln1_b, q_b, v_b, out_b, ln2_g, ln2_b, down_b)])
    unit, factor = normalized(x.astype(F32))
    h1 = (unit * vec[0:1] + vec[1:2]).astype(BF16)
    bias = jnp.concatenate([vec[2], jnp.zeros_like(vec[2]), vec[3]])
    qkv = (dot_on(h1, qkv_w, 1, 0) + bias).astype(BF16).reshape(groups, seq_rows, 3 * D)
    attended, row_side = attention(lengths, qkv)
    act, up_g, down_g, out_g, attended_g, mid_g, sums, up_sum = feed_forward(
        attended.reshape(count, D),
        x,
        cotangent.reshape(count, D),
        out_w,
        vec,
        up_b.astype(F32)[None],
        up_w,
        down_w,
    )
    dqkv = attention_back(
        lengths, qkv, attended, row_side, attended_g.reshape(groups, seq_rows, D)
    ).reshape(count, 3 * D)
    qkv_g = dot_on(h1, dqkv, 0, 0)
    columns = jnp.sum(dqkv.astype(F32), 0)
    dh1 = dot_on(dqkv, qkv_w, 1, 1)
    input_g = mid_g + norm_back(dh1 * vec[0:1], unit, factor)
    weight_grads = distribute(
        (
            jnp.sum(dh1 * unit, 0),
            jnp.sum(dh1, 0),
            qkv_g,
            columns[:D],
            columns[2 * D :],
            out_g,
            sums[0],
            sums[1],
            sums[2],
            up_g,
            up_sum[0],
            down_g,
            sums[3],
        ),
        devices,
    )
    return (act.reshape(inputs.shape), input_g.reshape(inputs.shape)) + weight_grads


def solution(mesh):
    in_specs = (
        P(("batch", "seq"), None, None),
        P(("batch", "seq")),
        P(("batch", "seq"), None, None),
        P(("batch", "seq")),
        P(("batch", "seq")),
        P(("batch", "seq"), None),
        P(("batch", "seq")),
        P(("batch", "seq")),
        P(("batch", "seq"), None),
        P(("batch", "seq")),
        P(("batch", "seq")),
        P(("batch", "seq")),
        P(("batch", "seq"), None),
        P(("batch", "seq")),
        P(("batch", "seq"), None),
        P(("batch", "seq")),
    )
    out_specs = (
        P(("batch", "seq"), None, None),
        P(("batch", "seq"), None, None),
        P(("batch", "seq")),
        P(("batch", "seq")),
        P(("batch", "seq"), None),
        P(("batch", "seq")),
        P(("batch", "seq")),
        P(("batch", "seq"), None),
        P(("batch", "seq")),
        P(("batch", "seq")),
        P(("batch", "seq")),
        P(("batch", "seq"), None),
        P(("batch", "seq")),
        P(("batch", "seq"), None),
        P(("batch", "seq")),
    )
    body = functools.partial(shards, mesh.size)
    return jax.shard_map(body, mesh=mesh, in_specs=in_specs, out_specs=out_specs, check_vma=False)
```

```python
import functools

import jax
import jax.numpy as jnp
from jax import lax
from jax.experimental import pallas as pl
from jax.experimental.pallas import tpu as pltpu
from jax.sharding import PartitionSpec as P


D = 768
HEADS = 12
HEAD_DIM = 64


EPS = 1e-06


GRID = (4, 2, 2, 2)
TILE = (16, 128)


def cut_of(cols):
    return max(128, (cols * 2 // 9 + 64) // 128 * 128) if cols > 128 else 0


F32, BF16 = jnp.float32, jnp.bfloat16
PAIR = 2 * HEAD_DIM


def dot_on(left, right, dim_left, dim_right):
    return lax.dot_general(
        left, right, (((dim_left,), (dim_right,)), ((), ())), preferred_element_type=F32
    )


def lane_of(rows):
    return lax.broadcasted_iota(jnp.int32, (rows, PAIR), 1)


def key_lanes(rows, length):
    lane = lax.rem(lane_of(rows), HEAD_DIM)
    position = lax.broadcasted_iota(jnp.int32, (rows, PAIR), 0)
    bias = jnp.where(position < length, 0.0, -1e30)
    return jnp.where(lane < 3, 1.0, jnp.where(lane == 3, bias, 0.0)).astype(BF16)


def row_lanes(first_head, second_head, one):
    lane = lane_of(first_head.shape[0])
    place = lax.rem(lane, HEAD_DIM)
    value = jnp.where(lane < HEAD_DIM, second_head, first_head)
    high = value.astype(BF16).astype(F32)
    rest = value - high
    middle = rest.astype(BF16).astype(F32)
    low = rest - middle
    tail = jnp.where(place == 2, low, jnp.where(place == 3, one, 0.0))
    return jnp.where(place == 0, high, jnp.where(place == 1, middle, tail)).astype(BF16)


def pair_columns(pair):
    return [pl.ds(pl.multiple_of(part * D + pair * PAIR, PAIR), PAIR) for part in range(3)]


def attend_pair(seq, pair, qkv, key_side, attended, row_side):
    here, keys_at, values_at = pair_columns(pair)
    queries = qkv[seq, :, here] * jnp.asarray(HEAD_DIM ** (-0.5), BF16)
    keys, values, side = qkv[seq, :, keys_at], qkv[seq, :, values_at], key_side[...]
    lane = lane_of(queries.shape[0])
    first = lane < HEAD_DIM
    one = (lax.rem(lane, HEAD_DIM) == 3).astype(F32).astype(BF16)
    zero = jnp.zeros_like(values)
    total, logs = None, []
    for head in range(2):
        mine = first if head == 0 else ~first
        scores = dot_on(jnp.where(mine, queries, one), jnp.where(mine, keys, side), 1, 1)
        peak = jnp.max(scores, 1, keepdims=True)
        terms = jnp.exp(scores - peak)
        weight = jnp.sum(terms, 1, keepdims=True)
        logs.append(-(peak + jnp.log(weight)))
        part = dot_on(terms.astype(BF16), jnp.where(mine, values, zero), 1, 0) * (1.0 / weight)
        total = part if total is None else total + part
    attended[seq, :, here] = total.astype(BF16)
    row_side[seq, :, here] = row_lanes(logs[0], logs[1], 1.0)


def attend_pair_back(seq, pair, qkv, key_side, attended, row_side, grad, out):
    here, keys_at, values_at = pair_columns(pair)
    scale = HEAD_DIM ** (-0.5)
    queries = qkv[seq, :, here] * jnp.asarray(scale, BF16)
    keys, values, side = qkv[seq, :, keys_at], qkv[seq, :, values_at], key_side[...]
    upper = grad[seq, :, here]
    rows = row_side[seq, :, here]
    first = lane_of(queries.shape[0]) < HEAD_DIM
    product_rows = upper.astype(F32) * attended[seq, :, here].astype(F32)
    sums = [
        jnp.sum(jnp.where(first, product_rows, 0.0), 1, keepdims=True),
        jnp.sum(jnp.where(first, 0.0, product_rows), 1, keepdims=True),
    ]
    minus = row_lanes(-sums[0], -sums[1], 0.0)
    zero = jnp.zeros_like(queries)
    results = [None] * 3
    for head in range(2):
        mine = first if head == 0 else ~first
        probs = jnp.exp(dot_on(jnp.where(mine, keys, side), jnp.where(mine, queries, rows), 1, 1))
        slope = dot_on(jnp.where(mine, values, side), jnp.where(mine, upper, minus), 1, 1)
        score_grad = (probs * slope).astype(BF16)
        parts = (
            dot_on(score_grad, jnp.where(mine, keys, zero), 0, 0),
            dot_on(score_grad, jnp.where(mine, queries, zero), 1, 0),
            dot_on(probs.astype(BF16), jnp.where(mine, upper, zero), 1, 0),
        )
        results = [new if old is None else old + new for old, new in zip(results, parts)]
    out[seq, :, here] = (results[0] * scale).astype(BF16)
    out[seq, :, keys_at] = results[1].astype(BF16)
    out[seq, :, values_at] = results[2].astype(BF16)


def attention(lengths, qkv):
    groups, rows = qkv.shape[:2]

    def body(lengths_ref, qkv_ref, attended, row_side, key_side):
        for seq in range(groups):
            key_side[...] = key_lanes(rows, lengths_ref[seq])

            @pl.loop(0, HEADS // 2)
            def _(pair):
                attend_pair(seq, pair, qkv_ref, key_side, attended, row_side)

    vmem = pl.BlockSpec(memory_space=pltpu.VMEM)
    return pl.pallas_call(
        body,
        out_shape=[jax.ShapeDtypeStruct((groups, rows, D), BF16)] * 2,
        in_specs=[pl.BlockSpec(memory_space=pltpu.SMEM), vmem],
        out_specs=[vmem] * 2,
        scratch_shapes=[pltpu.VMEM((rows, PAIR), BF16)],
        compiler_params=pltpu.CompilerParams(vmem_limit_bytes=40 << 20),
        name="attention",
    )(lengths, qkv)


def attention_back(lengths, qkv, attended, row_side, grad):
    groups, rows = qkv.shape[:2]

    def body(lengths_ref, qkv_ref, attended_ref, row_ref, grad_ref, out, key_side):
        for seq in range(groups):
            key_side[...] = key_lanes(rows, lengths_ref[seq])

            @pl.loop(0, HEADS // 2)
            def _(pair):
                attend_pair_back(seq, pair, qkv_ref, key_side, attended_ref, row_ref, grad_ref, out)

    vmem = pl.BlockSpec(memory_space=pltpu.VMEM)
    return pl.pallas_call(
        body,
        out_shape=jax.ShapeDtypeStruct(qkv.shape, BF16),
        in_specs=[pl.BlockSpec(memory_space=pltpu.SMEM)] + [vmem] * 4,
        out_specs=vmem,
        scratch_shapes=[pltpu.VMEM((rows, PAIR), BF16)],
        compiler_params=pltpu.CompilerParams(vmem_limit_bytes=40 << 20),
        name="attention_back",
    )(lengths, qkv, attended, row_side, grad)


FF_BLOCK = 512
ROW_BLOCK = 256


def normalized(rows):
    centered = rows - jnp.mean(rows, -1, keepdims=True)
    factor = lax.rsqrt(jnp.mean(centered * centered, -1, keepdims=True) + EPS)
    return centered * factor, factor


def norm_back(grad, unit, factor):
    return factor * (
        grad - jnp.mean(grad, -1, keepdims=True) - unit * jnp.mean(grad * unit, -1, keepdims=True)
    )


def ffn_body(
    attended, x, dy, out_w, vec, up_b, up_w, down_w,
    act_out, up_g, down_g, out_g, attended_g, mid_g, sums, up_sum,
    mid, h2, total, dh2, act, dpre, branch,
):
    step = pl.program_id(0)
    count = x.shape[0]
    blocks = count // ROW_BLOCK
    gain, shift = vec[5:6], vec[6:7]

    @pl.when(step == 0)
    def _():
        @pl.loop(0, blocks)
        def _(i):
            at = pl.ds(pl.multiple_of(i * ROW_BLOCK, ROW_BLOCK), ROW_BLOCK)
            rows = x[at].astype(F32) + (dot_on(attended[at], out_w[...], 1, 0) + vec[4:5])
            mid[at] = rows
            total[at] = rows + vec[7:8]
            h2[at] = (normalized(rows)[0] * gain + shift).astype(BF16)
            dh2[at] = jnp.zeros_like(rows)

    up_sum[...] = jnp.zeros_like(up_sum)

    @pl.loop(0, blocks)
    def _(i):
        at = pl.ds(pl.multiple_of(i * ROW_BLOCK, ROW_BLOCK), ROW_BLOCK)
        pre = dot_on(h2[at], up_w[...], 1, 0) + up_b[...]
        below = 0.5 * (1.0 + lax.erf(pre * 0.7071067811865476))
        low = (pre * below).astype(BF16)
        act[at] = low
        slope = below + pre * jnp.exp(-0.5 * pre * pre) * 0.3989422804014327
        grad = (dot_on(dy[at], down_w[...], 1, 1) * slope).astype(BF16)
        dpre[at] = grad
        up_sum[...] += jnp.sum(grad.astype(F32), 0, keepdims=True)
        total[at] += dot_on(low, down_w[...], 1, 0)
        dh2[at] += dot_on(grad, up_w[...], 1, 1)

    down_g[...] = dot_on(act[...], dy[...], 0, 0).astype(BF16)
    up_g[...] = dot_on(h2[...], dpre[...], 0, 0).astype(BF16)

    @pl.when(step == pl.num_programs(0) - 1)
    def _():
        sums[...] = jnp.zeros_like(sums)

        @pl.loop(0, blocks)
        def _(i):
            at = pl.ds(pl.multiple_of(i * ROW_BLOCK, ROW_BLOCK), ROW_BLOCK)
            act_out[at] = total[at].astype(BF16)
            unit, factor = normalized(mid[at])
            grad, upper = dh2[at], dy[at].astype(F32)
            rows = upper + norm_back(grad * gain, unit, factor)
            mid_g[at] = rows
            low = rows.astype(BF16)
            branch[at] = low
            attended_g[at] = dot_on(low, out_w[...], 1, 1).astype(BF16)
            for k, term in enumerate((low.astype(F32), grad * unit, grad, upper)):
                sums[k : k + 1] += jnp.sum(term, 0, keepdims=True)

        out_g[...] = dot_on(attended[...], branch[...], 0, 0).astype(BF16)


def feed_forward(attended, x, dy, out_w, vec, up_b, up_w, down_w):
    count, hidden = x.shape[0], up_w.shape[1]
    shape = jax.ShapeDtypeStruct

    def whole(*dims):
        return pl.BlockSpec(dims, lambda i: (0, 0), pipeline_mode=pl.Buffered(1))

    rows, square = whole(count, D), whole(D, D)
    by_column = pl.BlockSpec((D, FF_BLOCK), lambda i: (0, i))
    by_row = pl.BlockSpec((FF_BLOCK, D), lambda i: (i, 0))
    one_row = pl.BlockSpec((1, FF_BLOCK), lambda i: (0, i))
    vmem = pltpu.VMEM
    return pl.pallas_call(
        ffn_body,
        grid=(hidden // FF_BLOCK,),
        out_shape=[
            shape((count, D), BF16),
            shape((D, hidden), BF16),
            shape((hidden, D), BF16),
            shape((D, D), BF16),
            shape((count, D), BF16),
            shape((count, D), F32),
            shape((8, D), F32),
            shape((1, hidden), F32),
        ],
        in_specs=[rows, rows, rows, square, whole(*vec.shape), one_row, by_column, by_row],
        out_specs=[rows, by_column, by_row, square, rows, rows, whole(8, D), one_row],
        scratch_shapes=[
            vmem((count, D), F32),
            vmem((count, D), BF16),
            vmem((count, D), F32),
            vmem((count, D), F32),
            vmem((count, FF_BLOCK), BF16),
            vmem((count, FF_BLOCK), BF16),
            vmem((count, D), BF16),
        ],
        compiler_params=pltpu.CompilerParams(vmem_limit_bytes=56 << 20),
        name="feed_forward",
    )(attended, x, dy, out_w, vec, up_b, up_w, down_w)


MESH = pl.DeviceIdType.MESH
GATHER_SEMS = 27
REDUCE_SEMS = 27


class Where:
    def __init__(self):
        batch = lax.axis_index("batch")
        self.x = x = lax.axis_index("seq")
        self.z = z = batch // 4
        self.y = y = lax.rem(batch // 2, 2)
        self.c = c = lax.rem(batch, 2)
        self.other = 1 - c
        self.xp, self.yp = x + (1 - c) * (1 - 2 * x), y + c * (1 - 2 * y)
        self.xq, self.yq = x + c * (1 - 2 * x), y + (1 - c) * (1 - 2 * y)
        self.xr, self.yr = 1 - x, 1 - y
        self.zf, self.zb = lax.rem(z + 5 - 2 * c, 4), lax.rem(z + 3 + 2 * c, 4)
        self.zo = lax.rem(z + 2, 4)
        self.sibling = self.device(z, y, 1 - c, x)
        self.pn = self.device(z, self.yp, c, self.xp)
        self.qn = self.device(z, self.yq, c, self.xq)
        self.fn = self.device(self.zf, y, c, x)
        self.bn = self.device(self.zb, y, c, x)

    def device(self, z, y, c, x):
        return (z * 4 + y * 2 + c, x)

    def barrier(self):
        sem = pltpu.get_barrier_semaphore()
        for dev in (self.pn, self.qn, self.fn, self.bn, self.sibling):
            pl.semaphore_signal(sem, inc=1, device_id=dev, device_id_type=MESH)
        pl.semaphore_wait(sem, 5)


class Copies:
    def __init__(self, send, recv):
        self.send, self.recv, self.plans = send, recv, {}

    def build(self, key):
        index, plan = self.plans[key]
        source, target, dev = plan()
        return pltpu.make_async_remote_copy(
            src_ref=source,
            dst_ref=target,
            send_sem=self.send.at[index],
            recv_sem=self.recv.at[index],
            device_id=dev,
            device_id_type=MESH,
        )

    def start(self, key, plan):
        self.plans[key] = (len(self.plans), plan)
        self.build(key).start()

    def got(self, *keys):
        for key in keys:
            self.build(key).wait_recv()

    def drain(self):
        for key in self.plans:
            self.build(key).wait_send()


def gather_steps(w, src, full, send, recv, cut):
    cols = src.shape[1]
    low, high = pl.ds(0, cut), pl.ds(cut, cols - cut)
    z, y, c, x = w.z, w.y, w.c, w.x
    k = Copies(send, recv)
    every = slice(None)

    def local():
        return pltpu.make_async_copy(src, full.at[z, y, c, x], recv.at[GATHER_SEMS - 1])

    def mine(key, span, dev):
        k.start(key, lambda: (src.at[:, span], full.at[z, y, c, x, :, span], dev))

    def block(key, at, span, dev):
        def plan():
            ref = full.at[at + (slice(None), span)]
            return ref, ref, dev

        k.start(key, plan)

    def pass_on(key, zz, dev):
        block(key, (zz, y, c, x), high, dev)

    def start():
        mine("f", high, w.fn)
        mine("b", high, w.bn)
        if cut:
            mine("a1", low, w.pn)
            mine("a2", low, w.qn)
        mine("p0", high, w.pn)
        mine("q0", high, w.qn)
        local().start()

    def from_back():
        k.got("f")
        pass_on("ff", w.zb, w.fn)
        pass_on("p1", w.zb, w.pn)
        pass_on("q1", w.zb, w.qn)

    def from_front():
        k.got("b")
        pass_on("p2", w.zf, w.pn)
        pass_on("q2", w.zf, w.qn)

    def from_far():
        k.got("ff")
        pass_on("p3", w.zo, w.pn)
        pass_on("q3", w.zo, w.qn)

    def turn(n, zz):
        def run():
            k.got("p" + n)
            block("r" + n, (zz, w.yp, c, w.xp), high, w.qn)

        return run

    def share(n, zz):
        def run():
            if n == "0" and not cut:
                local().wait()
            k.got("q" + n, "r" + n)
            block("d" + n, (zz, every, c, every), high, w.sibling)

        return run

    def low_turn():
        k.got("a1")
        block("a3", (z, w.yp, c, w.xp), low, w.qn)

    def low_z():
        local().wait()
        k.got("a2", "a3")
        block("af", (z, every, c, every), low, w.fn)
        block("ab", (z, every, c, every), low, w.bn)

    def low_far():
        k.got("af")
        block("aff", (w.zb, every, c, every), low, w.fn)

    def low_share():
        k.got("ab", "aff")
        block("da", (every, every, c, every), low, w.sibling)

    def end():
        k.got("d0", "d1", "d2", "d3")
        if cut:
            k.got("da")

    steps = {"S": start, "B1": from_back, "B2": from_front, "B3": from_far, "E": end}
    for n, zz in (("0", z), ("1", w.zb), ("2", w.zf), ("3", w.zo)):
        steps["R" + n] = turn(n, zz)
        steps["D" + n] = share(n, zz)
    steps |= {"A2": low_turn, "A3": low_z, "A4": low_far, "DA": low_share}
    return steps, k.drain


def reduce_room(rows, cols, cut, dtype, hold):
    rest = cols - cut
    shapes = [(4, 2, 2, rows, cols)] * (2 if hold else 1)
    shapes += [(2, 4, rows, rest), (4, rows, rest), (3, rows, rest)]
    if cut:
        shapes += [(3, 2, 2, rows, cut), (3, rows, cut)]
    return [pltpu.VMEM(shape, dtype) for shape in shapes]


def reduce_steps(w, parts, both, out, room, send, recv, cut):
    rows, cols = out.shape
    held, room = (room[0], room[1:]) if both is None else (both.at[0], room)
    other, from_q, from_p, from_z = room[:4]
    if cut:
        low_z, low_pq = room[4:]
    low, high = pl.ds(0, cut), pl.ds(cut, cols - cut)
    z, y, x = w.z, w.y, w.x
    k = Copies(send, recv)
    pairs = [(a, b) for a in range(2) for b in range(2)]
    every = slice(None)

    def outgoing(zz, span):
        if both is None:
            return parts.at[zz, :, w.other, :, :, span]
        return both.at[1, zz, :, :, :, span]

    def local():
        return pltpu.make_async_copy(parts.at[:, :, w.c], held, recv.at[REDUCE_SEMS - 1])

    def add(target, term):
        target[...] += term[...]

    def total(mine, one, two):
        return mine.astype(F32) + one.astype(F32) + two.astype(F32)

    def to_sibling(key, zz, span):
        k.start(key, lambda: (outgoing(zz, span), other.at[zz, :, :, :, span], w.sibling))

    def add_sibling(zz, span):
        for a, b in pairs:
            add(held.at[zz, a, b, :, span], other.at[zz, a, b, :, span])

    def first():
        to_sibling("so", w.zo, high)
        if both is None:
            local().start()

    def rest():
        if cut:
            to_sibling("sa", every, low)
        to_sibling("sf", w.zb, high)
        to_sibling("sb", w.zf, high)
        to_sibling("sz", z, high)

    def to_q(n, zz):
        def run():
            if both is None and n == "o":
                local().wait()
            k.got("s" + n)
            add_sibling(zz, high)
            k.start("r" + n, lambda: (held.at[zz, w.yr, w.xr, :, high], from_q.at[1, zz], w.qn))
            k.start("q" + n, lambda: (held.at[zz, w.yq, w.xq, :, high], from_q.at[0, zz], w.qn))

        return run

    def to_p(n, zz):
        def run():
            k.got("r" + n)
            add(held.at[zz, w.yp, w.xp, :, high], from_q.at[1, zz])
            k.start("p" + n, lambda: (held.at[zz, w.yp, w.xp, :, high], from_p.at[zz], w.pn))

        return run

    def to_z(n, zz):
        def run():
            k.got("q" + n)
            add(held.at[zz, y, x, :, high], from_q.at[0, zz])
            k.got("p" + n)
            add(held.at[zz, y, x, :, high], from_p.at[zz])
            if n == "o":
                k.start("zo", lambda: (held.at[w.zo, y, x, :, high], from_z.at[0], w.fn))
            if n == "b":
                k.start("zb", lambda: (held.at[w.zb, y, x, :, high], from_z.at[1], w.bn))

        return run

    def relay():
        k.got("zo")
        add(held.at[w.zf, y, x, :, high], from_z.at[0])
        k.start("zf", lambda: (held.at[w.zf, y, x, :, high], from_z.at[2], w.fn))

    def finish():
        k.got("zb", "zf")
        out[:, high] = total(held[z, y, x, :, high], from_z[1], from_z[2])

    def low_first():
        k.got("sa")
        add_sibling(w.zo, low)
        k.start("ao", lambda: (held.at[w.zo, :, :, :, low], low_z.at[0], w.fn))
        add_sibling(w.zb, low)
        k.start("ab", lambda: (held.at[w.zb, :, :, :, low], low_z.at[1], w.bn))
        add_sibling(w.zf, low)
        add_sibling(z, low)

    def low_relay():
        k.got("ao")
        for a, b in pairs:
            add(held.at[w.zf, a, b, :, low], low_z.at[0, a, b])
        k.start("af", lambda: (held.at[w.zf, :, :, :, low], low_z.at[2], w.fn))

    def low_q():
        k.got("ab", "af")
        for a, b in pairs:
            block = held.at[z, a, b, :, low]
            block[...] = total(block[...], low_z[1, a, b], low_z[2, a, b]).astype(block.dtype)
        k.start("lr", lambda: (held.at[z, w.yr, w.xr, :, low], low_pq.at[0], w.qn))
        k.start("lq", lambda: (held.at[z, w.yq, w.xq, :, low], low_pq.at[1], w.qn))

    def low_p():
        k.got("lr")
        add(held.at[z, w.yp, w.xp, :, low], low_pq.at[0])
        k.start("lp", lambda: (held.at[z, w.yp, w.xp, :, low], low_pq.at[2], w.pn))

    def low_finish():
        k.got("lq", "lp")
        out[:, low] = total(held[z, y, x, :, low], low_pq[1], low_pq[2])

    steps = {"D": first, "E": rest, "ZF": relay, "OB": finish}
    for n, zz in (("o", w.zo), ("f", w.zf), ("b", w.zb), ("z", z)):
        steps["U" + n] = to_q(n, zz)
        steps["P" + n] = to_p(n, zz)
        steps["F" + n] = to_z(n, zz)
    steps |= {"LA": low_first, "LF": low_relay, "LQ": low_q, "LP": low_p, "OA": low_finish}
    return steps, k.drain


PART = 3 * 3 * PAIR


def run_schedule(schedule, action, loop_body):
    before, inside, after = schedule
    for name in before:
        action(name)()

    @pl.loop(0, HEADS)
    def _(i):
        for number, names in enumerate(inside):
            if names:

                @pl.when(i == number)
                def _():
                    for name in names:
                        action(name)()

        loop_body(i)

    for name in after:
        action(name)()


def split_index(shape, dim, width):
    index = lax.broadcasted_iota(jnp.int32, shape, dim).astype(F32)
    whole = jnp.floor((index + 0.5) * (1.0 / width))
    return whole, index - whole * width


def spread(values, width):
    rows, cols = values.shape
    owners = cols // width
    shape = (owners, rows, cols)
    whole, _ = split_index(shape, 2, width)
    owner = lax.broadcasted_iota(jnp.int32, shape, 0).astype(F32)
    picked = jnp.where(whole == owner, values[None], 0.0).reshape(owners * rows, cols)
    _, place = split_index((cols, TILE[1]), 0, width)
    lane = lax.broadcasted_iota(jnp.int32, (cols, TILE[1]), 1).astype(F32)
    fold = (place == lane).astype(F32).astype(BF16)
    high = picked.astype(BF16)
    rest = picked - high.astype(F32)
    middle = rest.astype(BF16)
    low = (rest - middle.astype(F32)).astype(BF16)
    tiles = sum(dot_on(part, fold, 1, 0) for part in (high, middle, low))
    return tiles.reshape(owners, rows, TILE[1])


REDUCED = "udoabs"


def backward_body(schedule, cuts, ends, *refs):
    lengths, vec, sums, up_sum = refs[:4]
    loads_from = refs[4:12]
    hbm_parts = refs[12:15]
    input_g, qkv_out, *outs = refs[15:21]
    loads_to = refs[21:28] + (input_g,)
    qkv, attended, row_side, grad, h1, x, qkv_w = loads_to[:7]
    dqkv, key_side, both_a, both_b, small, result_a, result_b, column_sums, send, recv, load = refs[28:39]
    rooms = refs[39:]
    rooms = [rooms[ends[i] : ends[i + 1]] for i in range(6)]
    count = x.shape[0]
    rows = qkv.shape[1]
    w = Where()
    w.barrier()

    def plan(i, parts, both, out):
        return reduce_steps(w, parts, both, out, rooms[i], send.at[i], recv.at[i], cuts[i])

    plans = [plan(i, hbm_parts[i], None, outs[i]) for i in range(3)]
    plans += [plan(3, None, both_a, result_a), plan(4, None, both_b, result_b), plan(5, None, small, outs[3])]
    flat = dqkv.reshape(count, 3 * D)

    def loading(i):
        return pltpu.make_async_copy(loads_from[i], loads_to[i], load.at[i])

    def start_loads():
        for i in range(8):
            loading(i).start()

    def prepare():
        small[...] = jnp.zeros_like(small)
        for seq in range(qkv.shape[0]):
            key_side[seq] = key_lanes(rows, lengths[seq])
        for i in range(8):
            loading(i).wait()

    def weight_grad(half, both):
        def run():
            for part in range(3):
                at = pl.ds(part * D + half * 3 * PAIR, 3 * PAIR)
                block = dot_on(h1[...], flat[:, at], 0, 0)
                size = D // 32
                for owner in range(32):
                    zz, yy, cc, xx = owner // 8, owner // 4 % 2, owner // 2 % 2, owner % 2
                    slot = w.other if cc else w.c
                    both[slot, zz, yy, xx, :, pl.ds(part * 3 * PAIR, 3 * PAIR)] = block[
                        owner * size : (owner + 1) * size
                    ].astype(BF16)

        return run

    def finish_rows(i):
        def run():
            at = pl.ds(i * ROW_BLOCK, ROW_BLOCK)
            terms = flat[at]
            grad_rows = dot_on(terms, qkv_w[...], 1, 1)
            unit, factor = normalized(x[at].astype(F32))
            input_g[at] += norm_back(grad_rows * vec[0:1], unit, factor)
            wide = terms.astype(F32)
            new = (grad_rows * unit, grad_rows, wide[:, :D], wide[:, 2 * D :])
            for k, term in enumerate(new):
                line = jnp.sum(term, 0, keepdims=True)
                column_sums[k : k + 1] = line if i == 0 else column_sums[k : k + 1] + line

        return run

    def small_sums():
        column_sums[4:8] = sums[0:4]
        small_tiles = spread(column_sums[...], D // 32).reshape(4, 2, 2, 2, 8, TILE[1])
        up_tiles = spread(up_sum[...], up_sum.shape[1] // 32).reshape(4, 2, 2, 2, 1, TILE[1])
        for cc in range(2):
            slot = w.other if cc else w.c
            small[slot, :, :, :, 0:8] = small_tiles[:, :, cc]
            small[slot, :, :, :, 8:9] = up_tiles[:, :, cc]

    actions = {"loads": start_loads, "ready": prepare, "small": small_sums}
    actions |= {"half0": weight_grad(0, both_a), "half1": weight_grad(1, both_b)}
    actions |= {"rows%d" % i: finish_rows(i) for i in range(count // ROW_BLOCK)}
    for name, (steps, _) in zip(REDUCED, plans):
        actions |= {name + step: run for step, run in steps.items()}

    def pair_back(i):
        pair, seq = i // 2, lax.rem(i, 2)
        attend_pair_back(seq, pair, qkv, key_side.at[seq], attended, row_side, grad, dqkv)

    run_schedule(schedule, actions.get, pair_back)
    for half, result in enumerate((result_a, result_b)):
        for part in range(3):
            at = pl.ds(part * 3 * PAIR, 3 * PAIR)
            qkv_out[:, pl.ds(part * D + half * 3 * PAIR, 3 * PAIR)] = result[:, at]
    for _, drain in plans:
        drain()


BACK_SCHEDULE = (
    ["uD", "dD", "oD", "uE", "dE", "oE", "loads", "uUo", "ready", "dUo", "oUo"],
    [
        [],
        ["uLA", "dLA"],
        ["oLA", "uUf"],
        ["dUf", "oUf", "uPo"],
        ["dPo", "oPo"],
        ["uUb", "dUb"],
        ["oUb", "uFo", "dFo", "half0", "aD", "aE", "oFo", "uPf", "dPf"],
        ["oPf", "aUo", "uLF", "dLF"],
        ["aLA", "oLF", "uUz", "aUf"],
        ["dUz", "oUz", "aPo"],
        ["uPb", "aUb", "dPb", "oPb"],
        ["aFo", "uFf", "dFf"],
    ],
    ["aPf", "oFf", "uZF", "aLF", "half1", "bD", "bE", "dZF", "oZF", "aUz", "uLQ", "dLQ", "aPb", "rows0", "oLQ",
        "bUo", "aFf", "uFb", "bLA", "rows1", "dFb", "aZF", "bUf", "oFb", "uPz", "rows2", "bPo", "aLQ", "dPz",
        "bUb", "oPz", "aFb", "rows3", "uLP", "bFo", "dLP", "aPz", "bPf", "small", "sD", "sE", "oLP", "bLF",
        "aLP", "uFz", "sUo", "dFz", "bUz", "aFz", "oFz", "sUf", "bPb", "uOB", "sPo", "aOB", "dOB", "bFf", "sUb",
        "oOB", "aOA", "bZF", "sFo", "uOA", "sPf", "bLQ", "dOA", "sUz", "oOA", "bFb", "sPb", "bPz", "sFf", "bLP",
        "sZF", "bFz", "sFb", "sPz", "bOB", "sFz", "bOA", "sOB"],
)


def backward(lengths, vec, sums, up_sum, loads, parts):
    qkv, x = loads[0], loads[5]
    count = x.shape[0]
    shapes = [(p.shape[0] // 32, p.shape[1]) for p in parts]
    own = D // 32
    shapes += [(own, PART), (own, PART), TILE]
    cuts = [cut_of(s[1]) for s in shapes]
    kinds = [BF16] * 5 + [F32]
    rooms = [reduce_room(*shapes[i], cuts[i], kinds[i], i < 3) for i in range(6)]
    ends = [0]
    for room in rooms:
        ends.append(ends[-1] + len(room))
    shape, vmem = jax.ShapeDtypeStruct, pltpu.VMEM
    here, far = pl.BlockSpec(memory_space=pltpu.VMEM), pl.BlockSpec(memory_space=pltpu.HBM)
    return pl.pallas_call(
        functools.partial(backward_body, BACK_SCHEDULE, cuts, ends),
        out_shape=[shape((count, D), F32), shape((own, 3 * D), F32)]
        + [shape(s, F32) for s in shapes[:3] + [TILE]],
        in_specs=[pl.BlockSpec(memory_space=pltpu.SMEM)] + [here] * 3 + [far] * 11,
        out_specs=[here] * 6,
        scratch_shapes=[vmem(a.shape, a.dtype) for a in loads[:7]]
        + [
            vmem(qkv.shape, BF16),
            vmem(qkv.shape[:2] + (PAIR,), BF16),
            vmem((2, 4, 2, 2, own, PART), BF16),
            vmem((2, 4, 2, 2, own, PART), BF16),
            vmem((2, 4, 2, 2) + TILE, F32),
            vmem((own, PART), F32),
            vmem((own, PART), F32),
            vmem((8, D), F32),
            pltpu.SemaphoreType.DMA((6, REDUCE_SEMS)),
            pltpu.SemaphoreType.DMA((6, REDUCE_SEMS)),
            pltpu.SemaphoreType.DMA((8,)),
        ]
        + sum(rooms, []),
        compiler_params=pltpu.CompilerParams(
            collective_id=1, has_side_effects=True, vmem_limit_bytes=62 << 20
        ),
        name="backward",
    )(
        lengths, vec, sums, up_sum, *loads, *[p.reshape(GRID + shapes[i]) for i, p in enumerate(parts)],
    )


def deliver(large, *arrays):
    *whole, tile = arrays
    widths = [D // 32] * 8 + [whole[1].shape[1] // 32]
    count = len(whole)

    def body(*refs):
        sources, targets = refs[: count + 2], refs[count + 2 :]
        targets[0][...] = sources[0][...]

        @pl.when(pl.program_id(0) == 0)
        def _():
            for source, target in zip(sources[1:], targets[1 : count + 1]):
                target[...] = source[...]
            for i, width in enumerate(widths):
                targets[count + 1 + i][...] = sources[count + 1][i : i + 1, :width]

    def once(a):
        return pl.BlockSpec(a, lambda i: (0, 0), pipeline_mode=pl.Buffered(1))

    moving = pl.BlockSpec((ROW_BLOCK, D), lambda i: (i, 0))
    fixed = [a.shape for a in whole]
    lines = [(1, width) for width in widths]
    out = pl.pallas_call(
        body,
        grid=(large.shape[0] // ROW_BLOCK,),
        out_shape=[jax.ShapeDtypeStruct(a.shape, a.dtype) for a in (large, *whole)]
        + [jax.ShapeDtypeStruct(a, F32) for a in lines],
        in_specs=[moving] + [once(a) for a in fixed + [tile.shape]],
        out_specs=[moving] + [once(a) for a in fixed + lines],
        name="deliver",
    )(large, *whole, tile)
    return out[: count + 1], [line.reshape(-1) for line in out[count + 1 :]]


def expand(tiles, width):
    owners = 32
    rows = tiles.shape[0] // owners
    cols = width * owners
    _, place = split_index((TILE[1], cols), 1, width)
    lane = lax.broadcasted_iota(jnp.int32, (TILE[1], cols), 0).astype(F32)
    copies = dot_on(tiles, (place == lane).astype(F32).astype(BF16), 1, 0).reshape(owners, rows, cols)
    whole, _ = split_index((owners, rows, cols), 2, width)
    owner = lax.broadcasted_iota(jnp.int32, (owners, rows, cols), 0).astype(F32)
    return jnp.sum(jnp.where(whole == owner, copies, 0.0), 0)


def pack_tile(line, width, long_width):
    lane = lax.broadcasted_iota(jnp.int32, (TILE[1], TILE[1]), 1).astype(F32)
    row = lax.broadcasted_iota(jnp.int32, TILE, 0).astype(F32)
    total = jnp.zeros(TILE, F32)
    for block in range(line.shape[0]):
        values = jnp.broadcast_to(line[block : block + 1].astype(F32), TILE)
        begin = float(block * TILE[1])
        at = lax.broadcasted_iota(jnp.int32, TILE, 1).astype(F32) + begin
        source = lax.broadcasted_iota(jnp.int32, (TILE[1], TILE[1]), 0).astype(F32) + begin
        vector = jnp.floor((at + 0.5) * (1.0 / width))
        short = jnp.where((vector == row) & (row < 8.0), values, 0.0)
        place = source - jnp.floor((source + 0.5) * (1.0 / width)) * width
        total += dot_on(short.astype(BF16), (place == lane).astype(F32).astype(BF16), 1, 0)
        long = jnp.where((row == 8.0) & (at >= 8.0 * width) & (at < 8.0 * width + long_width), values, 0.0)
        total += dot_on(long.astype(BF16), (source - 8.0 * width == lane).astype(F32).astype(BF16), 1, 0)
    return total.astype(BF16)


GATHERED = "vqoud"


def forward_body(schedule, cuts, *refs):
    lengths, line, x, *sources = refs[:7]
    vec, up_b = refs[7:9]
    stores_to = refs[9:13]
    fulls = refs[13:17]
    stores_from = refs[17:21]
    h1, qkv, attended, row_side = stores_from
    tile, tiles, qkv_w, key_side, send, recv, load, store = refs[21:]
    rows = qkv.shape[1]
    count = x.shape[0]
    w = Where()
    tile[...] = pack_tile(line, D // 32, up_b.shape[1] // 32)
    w.barrier()
    plans = [gather_steps(w, tile, tiles, send.at[0], recv.at[0], 0)]
    plans += [
        gather_steps(w, sources[i], fulls[i], send.at[i + 1], recv.at[i + 1], cuts[i]) for i in range(4)
    ]
    flat = qkv.reshape(count, 3 * D)
    size = D // 32

    def weights():
        return [
            pltpu.make_async_copy(
                fulls[0].at[i // 8, i // 4 % 2, i // 2 % 2, i % 2], qkv_w.at[pl.ds(size * i, size)], load.at[i]
            )
            for i in range(32)
        ]

    def storing(i):
        return pltpu.make_async_copy(stores_from[i], stores_to[i], store.at[i])

    def vectors():
        packed = tiles[...].reshape(-1, TILE[1])
        vec[...] = expand(packed, D // 32)[:8]
        total = packed.shape[0]
        row = lax.broadcasted_iota(jnp.int32, (32, total), 0) * TILE[0] + 8
        chosen = row == lax.broadcasted_iota(jnp.int32, (32, total), 1)
        up_b[...] = expand(
            dot_on(chosen.astype(F32).astype(BF16), packed, 1, 0).astype(BF16), up_b.shape[1] // 32
        )

    def norm():
        @pl.loop(0, count // ROW_BLOCK)
        def _(i):
            at = pl.ds(pl.multiple_of(i * ROW_BLOCK, ROW_BLOCK), ROW_BLOCK)
            unit, _ = normalized(x[at].astype(F32))
            h1[at] = (unit * vec[0:1] + vec[1:2]).astype(BF16)

        storing(0).start()

    def project(part):
        def run():
            @pl.loop(0, count // ROW_BLOCK)
            def _(i):
                at = pl.ds(pl.multiple_of(i * ROW_BLOCK, ROW_BLOCK), ROW_BLOCK)
                to = pl.ds(part * D, D)
                result = dot_on(h1[at], qkv_w[:, to], 1, 0)
                if part != 1:
                    result = result + vec[2 + part // 2 : 3 + part // 2]
                flat[at, to] = result.astype(BF16)

            if part == 2:
                storing(1).start()

        return run

    def sides():
        for seq in range(qkv.shape[0]):
            key_side[seq] = key_lanes(rows, lengths[seq])

    def stores():
        storing(2).start()
        storing(3).start()

    actions = {
        "load": lambda: [copy.start() for copy in weights()],
        "loaded": lambda: [copy.wait() for copy in weights()],
        "vectors": vectors,
        "norm": norm,
        "sides": sides,
        "stores": stores,
    }
    actions |= {"project%d" % i: project(i) for i in range(3)}
    for name, (steps, _) in zip(GATHERED, plans):
        actions |= {name + step: run for step, run in steps.items()}

    def pair_forward(i):
        attend_pair(lax.rem(i, 2), i // 2, qkv, key_side.at[lax.rem(i, 2)], attended, row_side)

    run_schedule(schedule, actions.get, pair_forward)
    for i in range(4):
        storing(i).wait()
    for _, drain in plans:
        drain()


FORE_SCHEDULE = (
    ["vS", "qS", "sides", "vB1", "vB2", "vR0", "qA2", "qR0", "qB1", "vR1", "vR2", "vD0", "qA3", "qB2", "vB3",
        "qD0", "qR1", "oS", "uS", "qB3", "dS", "vD1", "vD2", "qR2", "qA4", "vR3", "qD1", "oA2", "oR0", "uA2",
        "oB1", "oB2", "uR0", "uB1", "qR3", "dA2", "uB2", "dR0", "qD2", "vD3", "dB1", "oA3", "oD0", "uA3", "oR1",
        "oR2", "vE", "vectors", "dB2", "uD0", "uR1", "norm", "oB3", "qDA", "qD3", "dA3", "uB3", "uR2", "qE",
        "load", "loaded", "dB3", "oA4", "dD0", "project0", "dR1", "project1", "uA4", "oD1", "oD2", "dR2",
        "project2"],
    [
        [],
        ["oR3", "uD1"],
        ["dA4"],
        ["uR3"],
        ["oDA"],
        ["uD2"],
        ["dR3", "uDA"],
        [],
        ["dD1", "dDA"],
        ["dD2", "oD3"],
        ["uD3"],
        ["dD3"],
    ],
    ["oE", "stores", "uE", "dE"],
)


def forward(lengths, line, x, matrices):
    count, groups = x.shape[0], lengths.shape[0]
    rows = count // groups
    cuts = [cut_of(m.shape[1]) for m in matrices]
    hidden = matrices[2].shape[1]
    shape, vmem = jax.ShapeDtypeStruct, pltpu.VMEM
    here, far = pl.BlockSpec(memory_space=pltpu.VMEM), pl.BlockSpec(memory_space=pltpu.HBM)
    kept = [(count, D), (groups, rows, 3 * D), (groups, rows, D), (groups, rows, D)]
    vec, up_b, h1, qkv, attended, row_side, *fulls = pl.pallas_call(
        functools.partial(forward_body, FORE_SCHEDULE, cuts),
        out_shape=[shape((8, D), F32), shape((1, hidden), F32)]
        + [shape(s, BF16) for s in kept]
        + [shape(GRID + m.shape, BF16) for m in matrices],
        in_specs=[pl.BlockSpec(memory_space=pltpu.SMEM), here, here] + [far] * 4,
        out_specs=[here] * 2 + [far] * 8,
        scratch_shapes=[vmem(s, BF16) for s in kept]
        + [
            vmem(TILE, BF16),
            vmem(GRID + TILE, BF16),
            vmem((D, 3 * D), BF16),
            vmem((groups, rows, PAIR), BF16),
            pltpu.SemaphoreType.DMA((5, GATHER_SEMS)),
            pltpu.SemaphoreType.DMA((5, GATHER_SEMS)),
            pltpu.SemaphoreType.DMA((32,)),
            pltpu.SemaphoreType.DMA((4,)),
        ],
        compiler_params=pltpu.CompilerParams(
            collective_id=0, has_side_effects=True, vmem_limit_bytes=62 << 20
        ),
        name="forward",
    )(lengths, line, x, *matrices)
    return vec, up_b, h1, qkv, attended, row_side, [f.reshape(-1, f.shape[-1]) for f in fulls]


def staged(params, x, lengths, dy):
    ln1_g, ln1_b, qkv_w, q_b, v_b, out_w, out_b, ln2_g, ln2_b, up_w, up_b, down_w, down_b = params
    small = (ln1_g, ln1_b, q_b, v_b, out_b, ln2_g, ln2_b, down_b, up_b)
    starts = [sum(v.shape[0] for v in small[:i]) for i in range(len(small) + 1)]
    blocks = -(-starts[-1] // TILE[1])
    line = sum(
        jnp.pad(v, (start, blocks * TILE[1] - start - v.shape[0])) for v, start in zip(small, starts)
    ).reshape(blocks, TILE[1])
    vec, up_full, h1, qkv, attended, row_side, (qkv_w, out_w, up_w, down_w) = forward(
        lengths, line, x, (qkv_w, out_w, up_w, down_w)
    )
    act, up_g, down_g, out_g, attended_g, mid_g, sums, up_sum = feed_forward(
        attended.reshape(x.shape), x, dy, out_w, vec, up_full, up_w, down_w
    )
    loads = (qkv, attended, row_side, attended_g.reshape(attended.shape), h1, x, qkv_w, mid_g)
    results = deliver(*backward(lengths, vec, sums, up_sum, loads, (up_g, down_g, out_g)))
    input_g, qkv_g, up_g, down_g, out_g = results[0]
    ln1_gg, ln1_bg, q_bg, v_bg, out_bg, ln2_gg, ln2_bg, down_bg, up_bg = results[1]
    return (
        act, input_g, ln1_gg, ln1_bg, qkv_g, q_bg, v_bg, out_g, out_bg, ln2_gg, ln2_bg, up_g, up_bg, down_g, down_bg
    )


def plain(params, x, lengths, dy):
    axes = ("batch", "seq")
    ln1_g, ln1_b, qkv_w, q_b, v_b, out_w, out_b, ln2_g, ln2_b, up_w, up_b, down_w, down_b = (
        lax.all_gather(p, axes, axis=0, tiled=True) for p in params
    )
    groups = lengths.shape[0]
    vec = jnp.stack([v.astype(F32) for v in (ln1_g, ln1_b, q_b, v_b, out_b, ln2_g, ln2_b, down_b)])
    unit, factor = normalized(x.astype(F32))
    h1 = (unit * vec[0:1] + vec[1:2]).astype(BF16)
    bias = jnp.concatenate([vec[2], jnp.zeros_like(vec[2]), vec[3]])
    qkv = (dot_on(h1, qkv_w, 1, 0) + bias).astype(BF16).reshape(groups, -1, 3 * D)
    attended, row_side = attention(lengths, qkv)
    act, up_g, down_g, out_g, attended_g, mid_g, sums, up_sum = feed_forward(
        attended.reshape(x.shape), x, dy, out_w, vec, up_b.astype(F32)[None], up_w, down_w
    )
    dqkv = attention_back(lengths, qkv, attended, row_side, attended_g.reshape(attended.shape))
    dqkv = dqkv.reshape(-1, 3 * D)
    qkv_g = dot_on(h1, dqkv, 0, 0)
    columns = jnp.sum(dqkv.astype(F32), 0)
    dh1 = dot_on(dqkv, qkv_w, 1, 1)
    input_g = mid_g + norm_back(dh1 * vec[0:1], unit, factor)
    grads = (
        jnp.sum(dh1 * unit, 0),
        jnp.sum(dh1, 0),
        qkv_g,
        columns[:D],
        columns[2 * D :],
        out_g,
        sums[0],
        sums[1],
        sums[2],
        up_g,
        up_sum[0],
        down_g,
        sums[3],
    )
    return act, input_g, *(
        lax.psum_scatter(g.astype(F32), axes, scatter_dimension=0, tiled=True) for g in grads
    )


def shards(
    devices,
    inputs,
    lengths,
    cotangent,
    ln1_gain,
    ln1_bias,
    qkv_weight,
    q_bias,
    v_bias,
    out_weight,
    out_bias,
    ln2_gain,
    ln2_bias,
    up_weight,
    up_bias,
    down_weight,
    down_bias,
):
    params = (
        ln1_gain,
        ln1_bias,
        qkv_weight,
        q_bias,
        v_bias,
        out_weight,
        out_bias,
        ln2_gain,
        ln2_bias,
        up_weight,
        up_bias,
        down_weight,
        down_bias,
    )
    groups, seq_rows = inputs.shape[:2]
    count = groups * seq_rows
    x, dy = inputs.reshape(count, D), cotangent.reshape(count, D)
    if devices == 32:
        act, input_g, *grads = staged(params, x, lengths, dy)
    else:
        act, input_g, *grads = plain(params, x, lengths, dy)
    return (act.reshape(inputs.shape), input_g.reshape(inputs.shape), *grads)


def solution(mesh):
    in_specs = (
        P(("batch", "seq"), None, None),
        P(("batch", "seq")),
        P(("batch", "seq"), None, None),
        P(("batch", "seq")),
        P(("batch", "seq")),
        P(("batch", "seq"), None),
        P(("batch", "seq")),
        P(("batch", "seq")),
        P(("batch", "seq"), None),
        P(("batch", "seq")),
        P(("batch", "seq")),
        P(("batch", "seq")),
        P(("batch", "seq"), None),
        P(("batch", "seq")),
        P(("batch", "seq"), None),
        P(("batch", "seq")),
    )
    out_specs = (
        P(("batch", "seq"), None, None),
        P(("batch", "seq"), None, None),
        P(("batch", "seq")),
        P(("batch", "seq")),
        P(("batch", "seq"), None),
        P(("batch", "seq")),
        P(("batch", "seq")),
        P(("batch", "seq"), None),
        P(("batch", "seq")),
        P(("batch", "seq")),
        P(("batch", "seq")),
        P(("batch", "seq"), None),
        P(("batch", "seq")),
        P(("batch", "seq"), None),
        P(("batch", "seq")),
    )
    body = functools.partial(shards, mesh.size)
    return jax.shard_map(body, mesh=mesh, in_specs=in_specs, out_specs=out_specs, check_vma=False)
```

```python
import functools

import jax
import jax.numpy as jnp
from jax import lax
from jax.experimental import pallas as pl
from jax.experimental.pallas import tpu as pltpu
from jax.sharding import PartitionSpec as P


D = 768
HEADS = 12
HEAD_DIM = 64


EPS = 1e-06


GRID = (4, 2, 2, 2)
TILE = (16, 128)


def cut_of(cols):
    return max(128, (cols * 2 // 9 + 64) // 128 * 128) if cols > 128 else 0


F32, BF16 = jnp.float32, jnp.bfloat16
PAIR = 2 * HEAD_DIM


def dot_on(left, right, dim_left, dim_right):
    return lax.dot_general(
        left, right, (((dim_left,), (dim_right,)), ((), ())), preferred_element_type=F32
    )


def lane_of(rows):
    return lax.broadcasted_iota(jnp.int32, (rows, PAIR), 1)


def key_lanes(rows, length):
    lane = lax.rem(lane_of(rows), HEAD_DIM)
    position = lax.broadcasted_iota(jnp.int32, (rows, PAIR), 0)
    bias = jnp.where(position < length, 0.0, -1e30)
    return jnp.where(lane < 3, 1.0, jnp.where(lane == 3, bias, 0.0)).astype(BF16)


def row_lanes(first_head, second_head, one):
    lane = lane_of(first_head.shape[0])
    place = lax.rem(lane, HEAD_DIM)
    value = jnp.where(lane < HEAD_DIM, second_head, first_head)
    high = value.astype(BF16).astype(F32)
    rest = value - high
    middle = rest.astype(BF16).astype(F32)
    low = rest - middle
    tail = jnp.where(place == 2, low, jnp.where(place == 3, one, 0.0))
    return jnp.where(place == 0, high, jnp.where(place == 1, middle, tail)).astype(BF16)


def pair_columns(pair):
    return [pl.ds(pl.multiple_of(part * D + pair * PAIR, PAIR), PAIR) for part in range(3)]


def attend_pair(seq, pair, qkv, key_side, attended, row_side):
    here, keys_at, values_at = pair_columns(pair)
    queries = qkv[seq, :, here] * jnp.asarray(HEAD_DIM ** (-0.5), BF16)
    keys, values, side = qkv[seq, :, keys_at], qkv[seq, :, values_at], key_side[...]
    lane = lane_of(queries.shape[0])
    first = lane < HEAD_DIM
    one = (lax.rem(lane, HEAD_DIM) == 3).astype(F32).astype(BF16)
    zero = jnp.zeros_like(values)
    total, logs = None, []
    for head in range(2):
        mine = first if head == 0 else ~first
        scores = dot_on(jnp.where(mine, queries, one), jnp.where(mine, keys, side), 1, 1)
        peak = jnp.max(scores, 1, keepdims=True)
        terms = jnp.exp(scores - peak)
        weight = jnp.sum(terms, 1, keepdims=True)
        logs.append(-(peak + jnp.log(weight)))
        part = dot_on(terms.astype(BF16), jnp.where(mine, values, zero), 1, 0) * (1.0 / weight)
        total = part if total is None else total + part
    attended[seq, :, here] = total.astype(BF16)
    row_side[seq, :, here] = row_lanes(logs[0], logs[1], 1.0)


def attend_pair_back(seq, pair, qkv, key_side, attended, row_side, grad, out):
    here, keys_at, values_at = pair_columns(pair)
    scale = HEAD_DIM ** (-0.5)
    queries = qkv[seq, :, here] * jnp.asarray(scale, BF16)
    keys, values, side = qkv[seq, :, keys_at], qkv[seq, :, values_at], key_side[...]
    upper = grad[seq, :, here]
    rows = row_side[seq, :, here]
    first = lane_of(queries.shape[0]) < HEAD_DIM
    product_rows = upper.astype(F32) * attended[seq, :, here].astype(F32)
    sums = [
        jnp.sum(jnp.where(first, product_rows, 0.0), 1, keepdims=True),
        jnp.sum(jnp.where(first, 0.0, product_rows), 1, keepdims=True),
    ]
    minus = row_lanes(-sums[0], -sums[1], 0.0)
    zero = jnp.zeros_like(queries)
    results = [None] * 3
    for head in range(2):
        mine = first if head == 0 else ~first
        probs = jnp.exp(dot_on(jnp.where(mine, keys, side), jnp.where(mine, queries, rows), 1, 1))
        slope = dot_on(jnp.where(mine, values, side), jnp.where(mine, upper, minus), 1, 1)
        score_grad = (probs * slope).astype(BF16)
        parts = (
            dot_on(score_grad, jnp.where(mine, keys, zero), 0, 0),
            dot_on(score_grad, jnp.where(mine, queries, zero), 1, 0),
            dot_on(probs.astype(BF16), jnp.where(mine, upper, zero), 1, 0),
        )
        results = [new if old is None else old + new for old, new in zip(results, parts)]
    out[seq, :, here] = (results[0] * scale).astype(BF16)
    out[seq, :, keys_at] = results[1].astype(BF16)
    out[seq, :, values_at] = results[2].astype(BF16)


def attention(lengths, qkv):
    groups, rows = qkv.shape[:2]

    def body(lengths_ref, qkv_ref, attended, row_side, key_side):
        for seq in range(groups):
            key_side[...] = key_lanes(rows, lengths_ref[seq])

            @pl.loop(0, HEADS // 2)
            def _(pair):
                attend_pair(seq, pair, qkv_ref, key_side, attended, row_side)

    vmem = pl.BlockSpec(memory_space=pltpu.VMEM)
    return pl.pallas_call(
        body,
        out_shape=[jax.ShapeDtypeStruct((groups, rows, D), BF16)] * 2,
        in_specs=[pl.BlockSpec(memory_space=pltpu.SMEM), vmem],
        out_specs=[vmem] * 2,
        scratch_shapes=[pltpu.VMEM((rows, PAIR), BF16)],
        compiler_params=pltpu.CompilerParams(vmem_limit_bytes=40 << 20),
        name="attention",
    )(lengths, qkv)


def attention_back(lengths, qkv, attended, row_side, grad):
    groups, rows = qkv.shape[:2]

    def body(lengths_ref, qkv_ref, attended_ref, row_ref, grad_ref, out, key_side):
        for seq in range(groups):
            key_side[...] = key_lanes(rows, lengths_ref[seq])

            @pl.loop(0, HEADS // 2)
            def _(pair):
                attend_pair_back(seq, pair, qkv_ref, key_side, attended_ref, row_ref, grad_ref, out)

    vmem = pl.BlockSpec(memory_space=pltpu.VMEM)
    return pl.pallas_call(
        body,
        out_shape=jax.ShapeDtypeStruct(qkv.shape, BF16),
        in_specs=[pl.BlockSpec(memory_space=pltpu.SMEM)] + [vmem] * 4,
        out_specs=vmem,
        scratch_shapes=[pltpu.VMEM((rows, PAIR), BF16)],
        compiler_params=pltpu.CompilerParams(vmem_limit_bytes=40 << 20),
        name="attention_back",
    )(lengths, qkv, attended, row_side, grad)


MESH = pl.DeviceIdType.MESH
GATHER_SEMS = 27
REDUCE_SEMS = 27


class Where:
    def __init__(self):
        batch = lax.axis_index("batch")
        self.x = x = lax.axis_index("seq")
        self.z = z = batch // 4
        self.y = y = lax.rem(batch // 2, 2)
        self.c = c = lax.rem(batch, 2)
        self.other = 1 - c
        self.xp, self.yp = x + (1 - c) * (1 - 2 * x), y + c * (1 - 2 * y)
        self.xq, self.yq = x + c * (1 - 2 * x), y + (1 - c) * (1 - 2 * y)
        self.xr, self.yr = 1 - x, 1 - y
        self.zf, self.zb = lax.rem(z + 5 - 2 * c, 4), lax.rem(z + 3 + 2 * c, 4)
        self.zo = lax.rem(z + 2, 4)
        self.sibling = self.device(z, y, 1 - c, x)
        self.pn = self.device(z, self.yp, c, self.xp)
        self.qn = self.device(z, self.yq, c, self.xq)
        self.fn = self.device(self.zf, y, c, x)
        self.bn = self.device(self.zb, y, c, x)
        self.rn = self.device(z, self.yr, c, self.xr)
        self.on = self.device(self.zo, y, c, x)

    def device(self, z, y, c, x):
        return (z * 4 + y * 2 + c, x)

    def barrier(self, *more):
        sem = pltpu.get_barrier_semaphore()
        for dev in (self.pn, self.qn, self.fn, self.bn, self.sibling) + more:
            pl.semaphore_signal(sem, inc=1, device_id=dev, device_id_type=MESH)
        pl.semaphore_wait(sem, 5 + len(more))


class Copies:
    def __init__(self, send, recv):
        self.send, self.recv, self.plans = send, recv, {}

    def build(self, key):
        index, plan = self.plans[key]
        source, target, dev = plan()
        return pltpu.make_async_remote_copy(
            src_ref=source,
            dst_ref=target,
            send_sem=self.send.at[index],
            recv_sem=self.recv.at[index],
            device_id=dev,
            device_id_type=MESH,
        )

    def step(self, needs, work, sends):
        for key, plan in sends:
            self.plans[key] = (len(self.plans), plan)

        def run():
            for key in needs.split():
                self.build(key).wait_recv()
            for piece in work:
                piece()
            for key, _ in sends:
                self.build(key).start()

        return run

    def drain(self):
        for key in self.plans:
            self.build(key).wait_send()


def gather_steps(w, src, full, send, recv, cut):
    cols = src.shape[1]
    low, high = pl.ds(0, cut), pl.ds(cut, cols - cut)
    z, y, c, x = w.z, w.y, w.c, w.x
    k = Copies(send, recv)
    every = slice(None)

    def local():
        return pltpu.make_async_copy(src, full.at[z, y, c, x], recv.at[GATHER_SEMS - 1])

    def local_start():
        local().start()

    def local_wait():
        local().wait()

    def mine(key, span, dev):
        return key, lambda: (src.at[:, span], full.at[z, y, c, x, :, span], dev)

    def block(key, at, span, dev):
        def plan():
            ref = full.at[at + (slice(None), span)]
            return ref, ref, dev

        return key, plan

    def on(key, zz, dev):
        return block(key, (zz, y, c, x), high, dev)

    own = [mine("f", high, w.fn), mine("b", high, w.bn)]
    if cut:
        own += [mine("a1", low, w.pn), mine("a2", low, w.qn)]
    own += [mine("p0", high, w.pn), mine("q0", high, w.qn)]
    share = (every, every, c, every)
    steps = [
        k.step("", [local_start], own),
        k.step("f", [], [on("ff", w.zb, w.fn), on("p1", w.zb, w.pn), on("q1", w.zb, w.qn)]),
        k.step("b", [], [on("p2", w.zf, w.pn), on("q2", w.zf, w.qn)]),
        k.step("ff", [], [on("p3", w.zo, w.pn), on("q3", w.zo, w.qn)]),
        k.step("d0 d1 d2 d3 da" if cut else "d0 d1 d2 d3", [], []),
    ]
    for n, zz in (("0", z), ("1", w.zb), ("2", w.zf), ("3", w.zo)):
        before = [local_wait] if n == "0" and not cut else []
        steps.append(k.step("p" + n, [], [block("r" + n, (zz, w.yp, c, w.xp), high, w.qn)]))
        steps.append(k.step("q%s r%s" % (n, n), before, [block("d" + n, (zz, every, c, every), high, w.sibling)]))
    if cut:
        here, back = (z, every, c, every), (w.zb, every, c, every)
        steps += [
            k.step("a1", [], [block("a3", (z, w.yp, c, w.xp), low, w.qn)]),
            k.step("a2 a3", [local_wait], [block("af", here, low, w.fn), block("ab", here, low, w.bn)]),
            k.step("af", [], [block("aff", back, low, w.fn)]),
            k.step("ab aff", [], [block("da", share, low, w.sibling)]),
        ]
    return steps, k.drain


def reduce_room(rows, cols, cut, dtype, hold):
    rest = cols - cut
    shapes = [(4, 2, 2, rows, cols)] * (2 if hold else 1)
    shapes += [(2, 4, rows, rest), (4, rows, rest), (3, rows, rest)]
    if cut:
        shapes += [(3, 2, 2, rows, cut), (3, rows, cut)]
    return [pltpu.VMEM(shape, dtype) for shape in shapes]


def reduce_steps(w, parts, both, out, room, send, recv, cut):
    rows, cols = out.shape
    held, room = (room[0], room[1:]) if both is None else (both.at[0], room)
    other, from_q, from_p, from_z = room[:4]
    if cut:
        low_z, low_pq = room[4:]
    low, high = pl.ds(0, cut), pl.ds(cut, cols - cut)
    z, y, x = w.z, w.y, w.x
    k = Copies(send, recv)
    pairs = [(a, b) for a in range(2) for b in range(2)]
    every = slice(None)

    def outgoing(zz, span):
        if both is None:
            return parts.at[zz, :, w.other, :, :, span]
        return both.at[1, zz, :, :, :, span]

    def local():
        return pltpu.make_async_copy(parts.at[:, :, w.c], held, recv.at[REDUCE_SEMS - 1])

    def local_start():
        if both is None:
            local().start()

    def local_wait():
        if both is None:
            local().wait()

    def add(where, what):
        def run():
            target, term = where(), what()
            target[...] += term[...]

        return run

    def total(mine, one, two):
        return mine.astype(F32) + one.astype(F32) + two.astype(F32)

    def to_sibling(key, zz, span):
        return key, lambda: (outgoing(zz, span), other.at[zz, :, :, :, span], w.sibling)

    def add_sibling(zz, span):
        def run():
            for a, b in pairs:
                held.at[zz, a, b, :, span][...] += other.at[zz, a, b, :, span][...]

        return run

    def at(zz, yy, xx, span):
        return lambda: held.at[zz, yy, xx, :, span]

    def sent(key, block, target, dev):
        return key, lambda: (block(), target(), dev)

    def finish():
        out[:, high] = total(held[z, y, x, :, high], from_z[1], from_z[2])

    to_z = {
        "o": [sent("zo", at(w.zo, y, x, high), lambda: from_z.at[0], w.fn)],
        "b": [sent("zb", at(w.zb, y, x, high), lambda: from_z.at[1], w.bn)],
    }
    rest = [to_sibling("sa", every, low)] if cut else []
    rest += [to_sibling("sf", w.zb, high), to_sibling("sb", w.zf, high), to_sibling("sz", z, high)]
    relay = sent("zf", at(w.zf, y, x, high), lambda: from_z.at[2], w.fn)
    steps = [
        k.step("", [local_start], [to_sibling("so", w.zo, high)]),
        k.step("", [], rest),
        k.step("zo", [add(at(w.zf, y, x, high), lambda: from_z.at[0])], [relay]),
        k.step("zb zf", [finish], []),
    ]

    def chain(n, zz):
        first = [local_wait] if n == "o" else []
        turned = at(zz, w.yp, w.xp, high)
        return [
            k.step(
                "s" + n,
                first + [add_sibling(zz, high)],
                [
                    sent("r" + n, at(zz, w.yr, w.xr, high), lambda: from_q.at[1, zz], w.qn),
                    sent("q" + n, at(zz, w.yq, w.xq, high), lambda: from_q.at[0, zz], w.qn),
                ],
            ),
            k.step(
                "r" + n,
                [add(turned, lambda: from_q.at[1, zz])],
                [sent("p" + n, turned, lambda: from_p.at[zz], w.pn)],
            ),
            k.step(
                "q%s p%s" % (n, n),
                [
                    add(at(zz, y, x, high), lambda: from_q.at[0, zz]),
                    add(at(zz, y, x, high), lambda: from_p.at[zz]),
                ],
                to_z.get(n, []),
            ),
        ]

    for n, zz in (("o", w.zo), ("f", w.zf), ("b", w.zb), ("z", z)):
        steps += chain(n, zz)
    if not cut:
        return steps, k.drain

    def low_relay():
        for a, b in pairs:
            held.at[w.zf, a, b, :, low][...] += low_z[0, a, b]

    def low_sum():
        for a, b in pairs:
            block = held.at[z, a, b, :, low]
            block[...] = total(block[...], low_z[1, a, b], low_z[2, a, b]).astype(block.dtype)

    def low_finish():
        out[:, low] = total(held[z, y, x, :, low], low_pq[1], low_pq[2])

    def low_block(zz):
        return lambda: held.at[zz, :, :, :, low]

    turned = at(z, w.yp, w.xp, low)
    steps += [
        k.step(
            "sa",
            [add_sibling(zz, low) for zz in (w.zo, w.zb, w.zf, z)],
            [
                sent("ao", low_block(w.zo), lambda: low_z.at[0], w.fn),
                sent("ab", low_block(w.zb), lambda: low_z.at[1], w.bn),
            ],
        ),
        k.step("ao", [low_relay], [sent("af", low_block(w.zf), lambda: low_z.at[2], w.fn)]),
        k.step(
            "ab af",
            [low_sum],
            [
                sent("lr", at(z, w.yr, w.xr, low), lambda: low_pq.at[0], w.qn),
                sent("lq", at(z, w.yq, w.xq, low), lambda: low_pq.at[1], w.qn),
            ],
        ),
        k.step(
            "lr", [add(turned, lambda: low_pq.at[0])], [sent("lp", turned, lambda: low_pq.at[2], w.pn)]
        ),
        k.step("lq lp", [low_finish], []),
    ]
    return steps, k.drain


def small_reduce_room(shape, dtype):
    return [pltpu.VMEM((4, 2, 2) + shape, dtype), pltpu.VMEM((3, 4) + shape, dtype), pltpu.VMEM((3,) + shape, dtype)]


def small_reduce_steps(w, both, out, room, send, recv):
    other, plane, ring = room
    held = both.at[0]
    z, y, x = w.z, w.y, w.x
    k = Copies(send, recv)

    def add_sibling():
        held[...] += other[...]

    def add_plane():
        held[:, y, x] = held[:, y, x] + plane[0] + plane[1] + plane[2]

    def add_ring():
        out[...] = held[z, y, x] + ring[0] + ring[1] + ring[2]

    def to_plane(key, yy, xx, slot, dev):
        return key, lambda: (held.at[:, yy, xx], plane.at[slot], dev)

    def to_ring(key, zz, slot, dev):
        return key, lambda: (held.at[zz, y, x], ring.at[slot], dev)

    steps = [
        k.step("", [], [("s", lambda: (both.at[1], other, w.sibling))]),
        k.step(
            "s",
            [add_sibling],
            [
                to_plane("r", w.yr, w.xr, 0, w.rn),
                to_plane("q", w.yq, w.xq, 1, w.qn),
                to_plane("p", w.yp, w.xp, 2, w.pn),
            ],
        ),
        k.step(
            "r q p",
            [add_plane],
            [to_ring("o", w.zo, 0, w.on), to_ring("f", w.zf, 1, w.fn), to_ring("b", w.zb, 2, w.bn)],
        ),
        k.step("o f b", [add_ring], []),
    ]
    return steps, k.drain


FF_BLOCK = 512
ROW_BLOCK = 256
FF_ROWS = 1024


def normalized(rows):
    centered = rows - jnp.mean(rows, -1, keepdims=True)
    factor = lax.rsqrt(jnp.mean(centered * centered, -1, keepdims=True) + EPS)
    return centered * factor, factor


def norm_back(grad, unit, factor):
    return factor * (
        grad - jnp.mean(grad, -1, keepdims=True) - unit * jnp.mean(grad * unit, -1, keepdims=True)
    )


def ffn_body(
    attended, x, dy, out_w, vec, up_b, up_w, down_w,
    act_out, up_g, down_g, out_g, attended_g, mid_g, sums, up_sum,
    mid, h2, total, dh2, act, dpre, branch,
):
    step = pl.program_id(0)
    count = x.shape[0]
    size = min(FF_ROWS, count)
    blocks = count // size
    gain, shift = vec[5:6], vec[6:7]

    @pl.when(step == 0)
    def _():
        @pl.loop(0, blocks)
        def _(i):
            at = pl.ds(pl.multiple_of(i * size, size), size)
            rows = x[at].astype(F32) + (dot_on(attended[at], out_w[...], 1, 0) + vec[4:5])
            mid[at] = rows
            total[at] = rows + vec[7:8]
            h2[at] = (normalized(rows)[0] * gain + shift).astype(BF16)
            dh2[at] = jnp.zeros_like(rows)

    up_sum[...] = jnp.zeros_like(up_sum)

    @pl.loop(0, blocks)
    def _(i):
        at = pl.ds(pl.multiple_of(i * size, size), size)
        pre = dot_on(h2[at], up_w[...], 1, 0) + up_b[...]
        below = 0.5 * (1.0 + lax.erf(pre * 0.7071067811865476))
        low = (pre * below).astype(BF16)
        act[at] = low
        slope = below + pre * jnp.exp(-0.5 * pre * pre) * 0.3989422804014327
        grad = (dot_on(dy[at], down_w[...], 1, 1) * slope).astype(BF16)
        dpre[at] = grad
        up_sum[...] += jnp.sum(grad.astype(F32), 0, keepdims=True)
        total[at] += dot_on(low, down_w[...], 1, 0)
        dh2[at] += dot_on(grad, up_w[...], 1, 1)

    down_g[...] = dot_on(act[...], dy[...], 0, 0).astype(BF16)
    up_g[...] = dot_on(h2[...], dpre[...], 0, 0).astype(BF16)

    @pl.when(step == pl.num_programs(0) - 1)
    def _():
        sums[...] = jnp.zeros_like(sums)

        @pl.loop(0, blocks)
        def _(i):
            at = pl.ds(pl.multiple_of(i * size, size), size)
            act_out[at] = total[at].astype(BF16)
            unit, factor = normalized(mid[at])
            grad, upper = dh2[at], dy[at].astype(F32)
            rows = upper + norm_back(grad * gain, unit, factor)
            mid_g[at] = rows
            low = rows.astype(BF16)
            branch[at] = low
            attended_g[at] = dot_on(low, out_w[...], 1, 1).astype(BF16)
            for k, term in enumerate((low.astype(F32), grad * unit, grad, upper)):
                sums[k : k + 1] += jnp.sum(term, 0, keepdims=True)

        out_g[...] = dot_on(attended[...], branch[...], 0, 0).astype(BF16)


def feed_forward(attended, x, dy, out_w, vec, up_b, up_w, down_w):
    count, hidden = x.shape[0], up_w.shape[1]
    shape = jax.ShapeDtypeStruct

    def whole(*dims):
        return pl.BlockSpec(dims, lambda i: (0, 0), pipeline_mode=pl.Buffered(1))

    rows, square = whole(count, D), whole(D, D)
    by_column = pl.BlockSpec((D, FF_BLOCK), lambda i: (0, i))
    by_row = pl.BlockSpec((FF_BLOCK, D), lambda i: (i, 0))
    one_row = pl.BlockSpec((1, FF_BLOCK), lambda i: (0, i))
    vmem = pltpu.VMEM
    return pl.pallas_call(
        ffn_body,
        grid=(hidden // FF_BLOCK,),
        out_shape=[
            shape((count, D), BF16),
            shape((D, hidden), BF16),
            shape((hidden, D), BF16),
            shape((D, D), BF16),
            shape((count, D), BF16),
            shape((count, D), F32),
            shape((8, D), F32),
            shape((1, hidden), F32),
        ],
        in_specs=[rows, rows, rows, square, whole(*vec.shape), one_row, by_column, by_row],
        out_specs=[rows, by_column, by_row, square, rows, rows, whole(8, D), one_row],
        scratch_shapes=[
            vmem((count, D), F32),
            vmem((count, D), BF16),
            vmem((count, D), F32),
            vmem((count, D), F32),
            vmem((count, FF_BLOCK), BF16),
            vmem((count, FF_BLOCK), BF16),
            vmem((count, D), BF16),
        ],
        compiler_params=pltpu.CompilerParams(vmem_limit_bytes=56 << 20),
        name="feed_forward",
    )(attended, x, dy, out_w, vec, up_b, up_w, down_w)


BACK_ROWS = 512
PART = 3 * 3 * PAIR


def run_schedule(schedule, plans, compute, loop_body):
    before, inside, after = schedule

    def run(codes):
        for code in codes:
            (compute[code - 1000] if code >= 1000 else plans[code // 32][0][code % 32])()

    run(before)

    @pl.loop(0, len(inside))
    def _(i):
        for number, codes in enumerate(inside):
            if codes:

                @pl.when(i == number)
                def _():
                    run(codes)

        loop_body(i)

    run(after)


def split_index(shape, dim, width):
    index = lax.broadcasted_iota(jnp.int32, shape, dim).astype(F32)
    whole = jnp.floor((index + 0.5) * (1.0 / width))
    return whole, index - whole * width


def spread(values, width):
    rows, cols = values.shape
    owners = cols // width
    shape = (owners, rows, cols)
    whole, _ = split_index(shape, 2, width)
    owner = lax.broadcasted_iota(jnp.int32, shape, 0).astype(F32)
    picked = jnp.where(whole == owner, values[None], 0.0).reshape(owners * rows, cols)
    _, place = split_index((cols, TILE[1]), 0, width)
    lane = lax.broadcasted_iota(jnp.int32, (cols, TILE[1]), 1).astype(F32)
    fold = (place == lane).astype(F32).astype(BF16)
    high = picked.astype(BF16)
    rest = picked - high.astype(F32)
    middle = rest.astype(BF16)
    low = (rest - middle.astype(F32)).astype(BF16)
    tiles = sum(dot_on(part, fold, 1, 0) for part in (high, middle, low))
    return tiles.reshape(owners, rows, TILE[1])


def backward_body(schedule, cuts, ends, *refs):
    lengths, vec, sums, up_sum = refs[:4]
    loads_from = refs[4:12]
    hbm_parts = refs[12:15]
    input_g, qkv_out, *outs = refs[15:21]
    loads_to = refs[21:28] + (input_g,)
    qkv, attended, row_side, grad, h1, x, qkv_w = loads_to[:7]
    dqkv, key_side, both_a, both_b, small, result_a, result_b, column_sums, send, recv, load = refs[28:39]
    rooms = refs[39:]
    rooms = [rooms[ends[i] : ends[i + 1]] for i in range(6)]
    count = x.shape[0]
    rows = qkv.shape[1]
    w = Where()
    w.barrier(w.rn, w.on)

    def plan(i, parts, both, out):
        return reduce_steps(w, parts, both, out, rooms[i], send.at[i], recv.at[i], cuts[i])

    plans = [plan(i, hbm_parts[i], None, outs[i]) for i in range(3)]
    plans += [plan(3, None, both_a, result_a), plan(4, None, both_b, result_b)]
    plans.append(small_reduce_steps(w, small, outs[3], rooms[5], send.at[5], recv.at[5]))
    flat = dqkv.reshape(count, 3 * D)

    def loading(i):
        return pltpu.make_async_copy(loads_from[i], loads_to[i], load.at[i])

    def start_loads(first, last):
        def run():
            for i in range(first, last):
                loading(i).start()

        return run

    def wait_loads(first, last):
        def run():
            for i in range(first, last):
                loading(i).wait()

        return run

    def prepare():
        small[...] = jnp.zeros_like(small)
        for seq in range(qkv.shape[0]):
            key_side[seq] = key_lanes(rows, lengths[seq])

    def weight_grad(half, both):
        def run():
            for part in range(3):
                at = pl.ds(part * D + half * 3 * PAIR, 3 * PAIR)
                block = dot_on(h1[...], flat[:, at], 0, 0)
                size = D // 32
                for owner in range(32):
                    zz, yy, cc, xx = owner // 8, owner // 4 % 2, owner // 2 % 2, owner % 2
                    slot = w.other if cc else w.c
                    both[slot, zz, yy, xx, :, pl.ds(part * 3 * PAIR, 3 * PAIR)] = block[
                        owner * size : (owner + 1) * size
                    ].astype(BF16)

        return run

    def finish_rows(i):
        def run():
            at = pl.ds(i * BACK_ROWS, BACK_ROWS)
            terms = flat[at]
            grad_rows = dot_on(terms, qkv_w[...], 1, 1)
            unit, factor = normalized(x[at].astype(F32))
            input_g[at] += norm_back(grad_rows * vec[0:1], unit, factor)
            wide = terms.astype(F32)
            new = (grad_rows * unit, grad_rows, wide[:, :D], wide[:, 2 * D :])
            for k, term in enumerate(new):
                line = jnp.sum(term, 0, keepdims=True)
                column_sums[k : k + 1] = line if i == 0 else column_sums[k : k + 1] + line

        return run

    def small_sums():
        column_sums[4:8] = sums[0:4]
        small_tiles = spread(column_sums[...], D // 32).reshape(4, 2, 2, 2, 8, TILE[1])
        up_tiles = spread(up_sum[...], up_sum.shape[1] // 32).reshape(4, 2, 2, 2, 1, TILE[1])
        for cc in range(2):
            slot = w.other if cc else w.c
            small[slot, :, :, :, 0:8] = small_tiles[:, :, cc]
            small[slot, :, :, :, 8:9] = up_tiles[:, :, cc]

    compute = [start_loads(0, 4), prepare, wait_loads(0, 4), start_loads(4, 8), wait_loads(4, 8)]
    compute += [weight_grad(0, both_a), weight_grad(1, both_b)]
    compute += [finish_rows(i) for i in range(count // BACK_ROWS)] + [small_sums]

    def pair_back(i):
        pair, seq = i // 2, lax.rem(i, 2)
        attend_pair_back(seq, pair, qkv, key_side.at[seq], attended, row_side, grad, dqkv)

    run_schedule(schedule, plans, compute, pair_back)
    for half, result in enumerate((result_a, result_b)):
        for part in range(3):
            at = pl.ds(part * 3 * PAIR, 3 * PAIR)
            qkv_out[:, pl.ds(part * D + half * 3 * PAIR, 3 * PAIR)] = result[:, at]
    for _, drain in plans:
        drain()


BACK_SCHEDULE = (
    [0, 32, 64, 1000, 1, 33, 65, 1001, 1002, 1003, 4, 36, 68],
    [
        [],
        [16, 48],
        [80, 7],
        [39, 71, 5],
        [37, 69],
        [10, 42],
        [74, 6, 38, 1004, 1005, 96, 97, 70, 8],
        [40, 100, 72],
        [17, 112, 49, 81, 103],
        [13, 45, 101],
        [77, 106, 11, 43],
        [102, 75, 9],
    ],
    [104, 41, 73, 113, 1006, 128, 129, 2, 34, 109, 1007, 66, 132, 18, 107, 144, 50, 82, 105, 135, 12, 1008, 133,
        98, 44, 138, 76, 114, 14, 134, 46, 1009, 160, 136, 108, 78, 145, 19, 110, 51, 141, 161, 83, 115, 139,
        15, 137, 162, 47, 111, 130, 79, 3, 99, 146, 163, 35, 140, 116, 67, 142, 20, 52, 147, 84, 143, 131, 148],
)


def backward(lengths, vec, sums, up_sum, loads, parts):
    qkv, x = loads[0], loads[5]
    count = x.shape[0]
    shapes = [(p.shape[0] // 32, p.shape[1]) for p in parts]
    own = D // 32
    shapes += [(own, PART), (own, PART), TILE]
    cuts = [cut_of(s[1]) for s in shapes]
    rooms = [reduce_room(*shapes[i], cuts[i], BF16, i < 3) for i in range(5)] + [small_reduce_room(TILE, F32)]
    ends = [0]
    for room in rooms:
        ends.append(ends[-1] + len(room))
    shape, vmem = jax.ShapeDtypeStruct, pltpu.VMEM
    here, far = pl.BlockSpec(memory_space=pltpu.VMEM), pl.BlockSpec(memory_space=pltpu.HBM)
    return pl.pallas_call(
        functools.partial(backward_body, BACK_SCHEDULE, cuts, ends),
        out_shape=[shape((count, D), F32), shape((own, 3 * D), F32)]
        + [shape(s, F32) for s in shapes[:3] + [TILE]],
        in_specs=[pl.BlockSpec(memory_space=pltpu.SMEM)] + [here] * 3 + [far] * 11,
        out_specs=[here] * 6,
        scratch_shapes=[vmem(a.shape, a.dtype) for a in loads[:7]]
        + [
            vmem(qkv.shape, BF16),
            vmem(qkv.shape[:2] + (PAIR,), BF16),
            vmem((2, 4, 2, 2, own, PART), BF16),
            vmem((2, 4, 2, 2, own, PART), BF16),
            vmem((2, 4, 2, 2) + TILE, F32),
            vmem((own, PART), F32),
            vmem((own, PART), F32),
            vmem((8, D), F32),
            pltpu.SemaphoreType.DMA((6, REDUCE_SEMS)),
            pltpu.SemaphoreType.DMA((6, REDUCE_SEMS)),
            pltpu.SemaphoreType.DMA((8,)),
        ]
        + sum(rooms, []),
        compiler_params=pltpu.CompilerParams(
            collective_id=1, has_side_effects=True, vmem_limit_bytes=62 << 20
        ),
        name="backward",
    )(
        lengths, vec, sums, up_sum, *loads, *[p.reshape(GRID + shapes[i]) for i, p in enumerate(parts)],
    )


def deliver(large, *arrays):
    *whole, tile = arrays
    widths = [D // 32] * 8 + [whole[1].shape[1] // 32]
    count = len(whole)

    def body(*refs):
        sources, targets = refs[: count + 2], refs[count + 2 :]
        targets[0][...] = sources[0][...]

        @pl.when(pl.program_id(0) == 0)
        def _():
            for source, target in zip(sources[1:], targets[1 : count + 1]):
                target[...] = source[...]
            for i, width in enumerate(widths):
                targets[count + 1 + i][...] = sources[count + 1][i : i + 1, :width]

    def once(a):
        return pl.BlockSpec(a, lambda i: (0, 0), pipeline_mode=pl.Buffered(1))

    moving = pl.BlockSpec((ROW_BLOCK, D), lambda i: (i, 0))
    fixed = [a.shape for a in whole]
    lines = [(1, width) for width in widths]
    out = pl.pallas_call(
        body,
        grid=(large.shape[0] // ROW_BLOCK,),
        out_shape=[jax.ShapeDtypeStruct(a.shape, a.dtype) for a in (large, *whole)]
        + [jax.ShapeDtypeStruct(a, F32) for a in lines],
        in_specs=[moving] + [once(a) for a in fixed + [tile.shape]],
        out_specs=[moving] + [once(a) for a in fixed + lines],
        name="deliver",
    )(large, *whole, tile)
    return out[: count + 1], [line.reshape(-1) for line in out[count + 1 :]]


def expand(tiles, width):
    owners = 32
    rows = tiles.shape[0] // owners
    cols = width * owners
    _, place = split_index((TILE[1], cols), 1, width)
    lane = lax.broadcasted_iota(jnp.int32, (TILE[1], cols), 0).astype(F32)
    copies = dot_on(tiles, (place == lane).astype(F32).astype(BF16), 1, 0).reshape(owners, rows, cols)
    whole, _ = split_index((owners, rows, cols), 2, width)
    owner = lax.broadcasted_iota(jnp.int32, (owners, rows, cols), 0).astype(F32)
    return jnp.sum(jnp.where(whole == owner, copies, 0.0), 0)


def pack_tile(line, width, long_width):
    lane = lax.broadcasted_iota(jnp.int32, (TILE[1], TILE[1]), 1).astype(F32)
    row = lax.broadcasted_iota(jnp.int32, TILE, 0).astype(F32)
    total = jnp.zeros(TILE, F32)
    for block in range(line.shape[0]):
        values = jnp.broadcast_to(line[block : block + 1].astype(F32), TILE)
        begin = float(block * TILE[1])
        at = lax.broadcasted_iota(jnp.int32, TILE, 1).astype(F32) + begin
        source = lax.broadcasted_iota(jnp.int32, (TILE[1], TILE[1]), 0).astype(F32) + begin
        vector = jnp.floor((at + 0.5) * (1.0 / width))
        short = jnp.where((vector == row) & (row < 8.0), values, 0.0)
        place = source - jnp.floor((source + 0.5) * (1.0 / width)) * width
        total += dot_on(short.astype(BF16), (place == lane).astype(F32).astype(BF16), 1, 0)
        long = jnp.where((row == 8.0) & (at >= 8.0 * width) & (at < 8.0 * width + long_width), values, 0.0)
        total += dot_on(long.astype(BF16), (source - 8.0 * width == lane).astype(F32).astype(BF16), 1, 0)
    return total.astype(BF16)


def forward_body(schedule, cuts, *refs):
    lengths, line, x, *sources = refs[:7]
    vec, up_b = refs[7:9]
    stores_to = refs[9:13]
    fulls = refs[13:17]
    stores_from = refs[17:21]
    h1, qkv, attended, row_side = stores_from
    tile, tiles, qkv_w, key_side, send, recv, load, store = refs[21:]
    rows = qkv.shape[1]
    count = x.shape[0]
    w = Where()
    tile[...] = pack_tile(line, D // 32, up_b.shape[1] // 32)
    w.barrier()
    plans = [gather_steps(w, tile, tiles, send.at[0], recv.at[0], 0)]
    plans += [
        gather_steps(w, sources[i], fulls[i], send.at[i + 1], recv.at[i + 1], cuts[i]) for i in range(4)
    ]
    flat = qkv.reshape(count, 3 * D)
    size = D // 32

    def weights():
        return [
            pltpu.make_async_copy(
                fulls[0].at[i // 8, i // 4 % 2, i // 2 % 2, i % 2], qkv_w.at[pl.ds(size * i, size)], load.at[i]
            )
            for i in range(32)
        ]

    def storing(i):
        return pltpu.make_async_copy(stores_from[i], stores_to[i], store.at[i])

    def vectors():
        packed = tiles[...].reshape(-1, TILE[1])
        vec[...] = expand(packed, D // 32)[:8]
        total = packed.shape[0]
        row = lax.broadcasted_iota(jnp.int32, (32, total), 0) * TILE[0] + 8
        chosen = row == lax.broadcasted_iota(jnp.int32, (32, total), 1)
        up_b[...] = expand(
            dot_on(chosen.astype(F32).astype(BF16), packed, 1, 0).astype(BF16), up_b.shape[1] // 32
        )

    def norm():
        @pl.loop(0, count // ROW_BLOCK)
        def _(i):
            at = pl.ds(pl.multiple_of(i * ROW_BLOCK, ROW_BLOCK), ROW_BLOCK)
            unit, _ = normalized(x[at].astype(F32))
            h1[at] = (unit * vec[0:1] + vec[1:2]).astype(BF16)

        storing(0).start()

    def project(part):
        def run():
            @pl.loop(0, count // ROW_BLOCK)
            def _(i):
                at = pl.ds(pl.multiple_of(i * ROW_BLOCK, ROW_BLOCK), ROW_BLOCK)
                to = pl.ds(part * D, D)
                result = dot_on(h1[at], qkv_w[:, to], 1, 0)
                if part != 1:
                    result = result + vec[2 + part // 2 : 3 + part // 2]
                flat[at, to] = result.astype(BF16)

            if part == 2:
                storing(1).start()

        return run

    def sides():
        for seq in range(qkv.shape[0]):
            key_side[seq] = key_lanes(rows, lengths[seq])

    def stores():
        storing(2).start()
        storing(3).start()

    def load_weights():
        for copy in weights():
            copy.start()

    def wait_weights():
        for copy in weights():
            copy.wait()

    compute = [sides, vectors, norm, load_weights, wait_weights, project(0), project(1), project(2), stores]

    def pair_forward(i):
        attend_pair(lax.rem(i, 2), i // 2, qkv, key_side.at[lax.rem(i, 2)], attended, row_side)

    run_schedule(schedule, plans, compute, pair_forward)
    for i in range(4):
        storing(i).wait()
    for _, drain in plans:
        drain()


FORE_SCHEDULE = (
    [0, 32, 1000, 1, 2, 5, 45, 37, 33, 7, 9, 6, 46, 34, 3, 38, 39, 35, 8, 10, 41, 47, 64, 96, 128, 11, 40, 43,
        42, 77, 48, 69, 65, 109, 66, 101, 141, 97, 133, 98, 12, 44, 78, 70, 71, 4, 1001, 129, 110, 73, 36, 1002,
        130, 142, 67, 103, 102, 1003, 1004, 1005, 99, 105, 79, 134, 1006, 72, 1007, 131, 135],
    [
        [],
        [111, 74],
        [137],
        [75],
        [],
        [143, 104],
        [107],
        [80],
        [106],
        [139, 112],
        [],
        [136, 144],
    ],
    [138, 76, 1008, 108, 140, 68, 100, 132],
)


def forward(lengths, line, x, matrices):
    count, groups = x.shape[0], lengths.shape[0]
    rows = count // groups
    cuts = [cut_of(m.shape[1]) for m in matrices]
    hidden = matrices[2].shape[1]
    shape, vmem = jax.ShapeDtypeStruct, pltpu.VMEM
    here, far = pl.BlockSpec(memory_space=pltpu.VMEM), pl.BlockSpec(memory_space=pltpu.HBM)
    kept = [(count, D), (groups, rows, 3 * D), (groups, rows, D), (groups, rows, D)]
    vec, up_b, h1, qkv, attended, row_side, *fulls = pl.pallas_call(
        functools.partial(forward_body, FORE_SCHEDULE, cuts),
        out_shape=[shape((8, D), F32), shape((1, hidden), F32)]
        + [shape(s, BF16) for s in kept]
        + [shape(GRID + m.shape, BF16) for m in matrices],
        in_specs=[pl.BlockSpec(memory_space=pltpu.SMEM), here, here] + [far] * 4,
        out_specs=[here] * 2 + [far] * 8,
        scratch_shapes=[vmem(s, BF16) for s in kept]
        + [
            vmem(TILE, BF16),
            vmem(GRID + TILE, BF16),
            vmem((D, 3 * D), BF16),
            vmem((groups, rows, PAIR), BF16),
            pltpu.SemaphoreType.DMA((5, GATHER_SEMS)),
            pltpu.SemaphoreType.DMA((5, GATHER_SEMS)),
            pltpu.SemaphoreType.DMA((32,)),
            pltpu.SemaphoreType.DMA((4,)),
        ],
        compiler_params=pltpu.CompilerParams(
            collective_id=0, has_side_effects=True, vmem_limit_bytes=62 << 20
        ),
        name="forward",
    )(lengths, line, x, *matrices)
    return vec, up_b, h1, qkv, attended, row_side, [f.reshape(-1, f.shape[-1]) for f in fulls]


def staged(params, x, lengths, dy):
    ln1_g, ln1_b, qkv_w, q_b, v_b, out_w, out_b, ln2_g, ln2_b, up_w, up_b, down_w, down_b = params
    small = (ln1_g, ln1_b, q_b, v_b, out_b, ln2_g, ln2_b, down_b, up_b)
    starts = [sum(v.shape[0] for v in small[:i]) for i in range(len(small) + 1)]
    blocks = -(-starts[-1] // TILE[1])
    line = sum(
        jnp.pad(v, (start, blocks * TILE[1] - start - v.shape[0])) for v, start in zip(small, starts)
    ).reshape(blocks, TILE[1])
    vec, up_full, h1, qkv, attended, row_side, (qkv_w, out_w, up_w, down_w) = forward(
        lengths, line, x, (qkv_w, out_w, up_w, down_w)
    )
    act, up_g, down_g, out_g, attended_g, mid_g, sums, up_sum = feed_forward(
        attended.reshape(x.shape), x, dy, out_w, vec, up_full, up_w, down_w
    )
    loads = (qkv, attended, row_side, attended_g.reshape(attended.shape), h1, x, qkv_w, mid_g)
    results = deliver(*backward(lengths, vec, sums, up_sum, loads, (up_g, down_g, out_g)))
    input_g, qkv_g, up_g, down_g, out_g = results[0]
    ln1_gg, ln1_bg, q_bg, v_bg, out_bg, ln2_gg, ln2_bg, down_bg, up_bg = results[1]
    return (
        act, input_g, ln1_gg, ln1_bg, qkv_g, q_bg, v_bg, out_g, out_bg, ln2_gg, ln2_bg, up_g, up_bg, down_g, down_bg
    )


def plain(params, x, lengths, dy):
    axes = ("batch", "seq")
    ln1_g, ln1_b, qkv_w, q_b, v_b, out_w, out_b, ln2_g, ln2_b, up_w, up_b, down_w, down_b = (
        lax.all_gather(p, axes, axis=0, tiled=True) for p in params
    )
    groups = lengths.shape[0]
    vec = jnp.stack([v.astype(F32) for v in (ln1_g, ln1_b, q_b, v_b, out_b, ln2_g, ln2_b, down_b)])
    unit, factor = normalized(x.astype(F32))
    h1 = (unit * vec[0:1] + vec[1:2]).astype(BF16)
    bias = jnp.concatenate([vec[2], jnp.zeros_like(vec[2]), vec[3]])
    qkv = (dot_on(h1, qkv_w, 1, 0) + bias).astype(BF16).reshape(groups, -1, 3 * D)
    attended, row_side = attention(lengths, qkv)
    act, up_g, down_g, out_g, attended_g, mid_g, sums, up_sum = feed_forward(
        attended.reshape(x.shape), x, dy, out_w, vec, up_b.astype(F32)[None], up_w, down_w
    )
    dqkv = attention_back(lengths, qkv, attended, row_side, attended_g.reshape(attended.shape))
    dqkv = dqkv.reshape(-1, 3 * D)
    qkv_g = dot_on(h1, dqkv, 0, 0)
    columns = jnp.sum(dqkv.astype(F32), 0)
    dh1 = dot_on(dqkv, qkv_w, 1, 1)
    input_g = mid_g + norm_back(dh1 * vec[0:1], unit, factor)
    grads = (
        jnp.sum(dh1 * unit, 0),
        jnp.sum(dh1, 0),
        qkv_g,
        columns[:D],
        columns[2 * D :],
        out_g,
        sums[0],
        sums[1],
        sums[2],
        up_g,
        up_sum[0],
        down_g,
        sums[3],
    )
    return act, input_g, *(
        lax.psum_scatter(g.astype(F32), axes, scatter_dimension=0, tiled=True) for g in grads
    )


def shards(
    devices,
    inputs,
    lengths,
    cotangent,
    ln1_gain,
    ln1_bias,
    qkv_weight,
    q_bias,
    v_bias,
    out_weight,
    out_bias,
    ln2_gain,
    ln2_bias,
    up_weight,
    up_bias,
    down_weight,
    down_bias,
):
    params = (
        ln1_gain,
        ln1_bias,
        qkv_weight,
        q_bias,
        v_bias,
        out_weight,
        out_bias,
        ln2_gain,
        ln2_bias,
        up_weight,
        up_bias,
        down_weight,
        down_bias,
    )
    groups, seq_rows = inputs.shape[:2]
    count = groups * seq_rows
    x, dy = inputs.reshape(count, D), cotangent.reshape(count, D)
    if devices == 32:
        act, input_g, *grads = staged(params, x, lengths, dy)
    else:
        act, input_g, *grads = plain(params, x, lengths, dy)
    return (act.reshape(inputs.shape), input_g.reshape(inputs.shape), *grads)


def solution(mesh):
    in_specs = (
        P(("batch", "seq"), None, None),
        P(("batch", "seq")),
        P(("batch", "seq"), None, None),
        P(("batch", "seq")),
        P(("batch", "seq")),
        P(("batch", "seq"), None),
        P(("batch", "seq")),
        P(("batch", "seq")),
        P(("batch", "seq"), None),
        P(("batch", "seq")),
        P(("batch", "seq")),
        P(("batch", "seq")),
        P(("batch", "seq"), None),
        P(("batch", "seq")),
        P(("batch", "seq"), None),
        P(("batch", "seq")),
    )
    out_specs = (
        P(("batch", "seq"), None, None),
        P(("batch", "seq"), None, None),
        P(("batch", "seq")),
        P(("batch", "seq")),
        P(("batch", "seq"), None),
        P(("batch", "seq")),
        P(("batch", "seq")),
        P(("batch", "seq"), None),
        P(("batch", "seq")),
        P(("batch", "seq")),
        P(("batch", "seq")),
        P(("batch", "seq"), None),
        P(("batch", "seq")),
        P(("batch", "seq"), None),
        P(("batch", "seq")),
    )
    body = functools.partial(shards, mesh.size)
    return jax.shard_map(body, mesh=mesh, in_specs=in_specs, out_specs=out_specs, check_vma=False)
```
